256 devices in a mesh: gx: 8 (over x, core), gy: 4 (over y), gz: 8 (over z).
Axes of the slice: x: 4, y: 4, z: 8, core: 2. Of those that a mesh axis runs over, the one named last changes fastest.
Arguments:
- charges: float32 [256, 1024, 1024], P('gz', 'gy', 'gx'), may hold values from -8 to 8
- fine_taps: float32 [2, 3, 17], replicated, may hold values from 0.05 to 0.45
- coarse_taps: float32 [2, 3, 17], replicated, may hold values from 0.05 to 0.45
Outputs:
- potential: float32 [256, 1024, 1024], P('gz', 'gy', 'gx')
The draws below stay inside these ranges and needn't reach their ends.
All inputs are finite; a program needn't handle non-finite values.
Results may differ from the reference program's by a relative error of at most 0.0003.
Values sent between devices are 32-bit elements; how exact they have to be, the bound alone decides.
No kernel may reach another device: no remote copies, remote signals or barrier semaphores. Data moves between devices by JAX's collectives and lax.ppermute only.
A program may use at most 128 MiB of HBM per device.

```python
import math
import jax
import jax.numpy as jnp
from jax import lax

RADIUS = 8
TERMS = 2
TOPB = 16
TAPS = 17
NX = 1024
NY = 1024
NZ = 256


def draw_charges(key, part):
    noise_key = jax.random.fold_in(key, 11)
    grid_shape = (NZ, NY, NX)
    return jax.random.truncated_normal(noise_key, -6.0, 6.0, grid_shape, jnp.float32)


def setup_inputs(seed: int = 0) -> dict:
    keys = jax.random.split(jax.random.key(seed), 4)
    return {
        "charges": draw_charges(jax.random.fold_in(keys[3], 71), 0),
        "fine_taps": jnp.clip(jax.random.uniform(keys[1], (TERMS, 3, TAPS), jnp.float32, 0.05, 0.45), 0.05, 0.45),
        "coarse_taps": jnp.clip(jax.random.uniform(keys[2], (TERMS, 3, TAPS), jnp.float32, 0.05, 0.45), 0.05, 0.45),
    }


def correlate(grid_field, tap_set):
    running = jnp.zeros(grid_field.shape, jnp.float32)
    for term_index in range(TERMS):
        current = grid_field
        for axis_pos, array_axis in ((0, 2), (1, 1), (2, 0)):
            summed = jnp.zeros(grid_field.shape, jnp.float32)
            for offset in range(-RADIUS, RADIUS + 1):
                summed = summed + tap_set[term_index, axis_pos, offset + RADIUS] * jnp.roll(current, -offset, axis=array_axis)
            current = summed
        running = running + current
    return running

def wrapped(anchor, target, period):
    distance = jnp.abs(anchor - target)
    return jnp.minimum(distance, period - distance).astype(jnp.float32)

def direct_top(top_grid):
    top_z, top_y, top_x = top_grid.shape
    cell_count = top_z * top_y * top_x
    flat_top = top_grid.reshape(-1)
    cell_ids = jnp.arange(cell_count, dtype=jnp.int32)
    z_cell = cell_ids // (top_y * top_x)
    y_cell = cell_ids // top_x % top_y
    x_cell = cell_ids % top_x
    row_block = math.gcd(cell_count, 512)

    def row_kernel(first_row):
        row_ids = first_row + jnp.arange(row_block, dtype=jnp.int32)
        dz = wrapped(row_ids[:, None] // (top_y * top_x), z_cell[None, :], top_z)
        dy = wrapped(row_ids[:, None] // top_x % top_y, y_cell[None, :], top_y)
        dx = wrapped(row_ids[:, None] % top_x, x_cell[None, :], top_x)
        kernel = 1.0 / (TOPB * TOPB * jnp.sqrt(1.0 + dz * dz + dy * dy + dx * dx))
        return jnp.dot(kernel, flat_top, precision=lax.Precision.HIGHEST)
    starts = jnp.arange(0, cell_count, row_block, dtype=jnp.int32)
    return lax.map(row_kernel, starts).reshape(top_grid.shape)

def expand(grid_field, factor):
    grid_field = jnp.repeat(grid_field, factor, axis=0)
    grid_field = jnp.repeat(grid_field, factor, axis=1)
    return jnp.repeat(grid_field, factor, axis=2)

def reference(charges, fine_taps, coarse_taps):
    fine_part = correlate(charges, fine_taps)
    coarse = charges.reshape(NZ // 2, 2, NY // 2, 2, NX // 2, 2).mean(axis=(1, 3, 5))
    coarse_part = correlate(coarse, coarse_taps)
    top_grid = coarse.reshape(NZ // (2 * TOPB), TOPB, NY // (2 * TOPB), TOPB, NX // (2 * TOPB), TOPB).sum(axis=(1, 3, 5))
    coarse_potential = coarse_part + expand(direct_top(top_grid), TOPB)
    return fine_part + expand(coarse_potential, 2)
```

```python
import functools
import itertools

import jax
import jax.numpy as jnp
from jax import lax
from jax.experimental import pallas as pl
from jax.experimental.pallas import tpu as pltpu
from jax.sharding import PartitionSpec as P

f32 = jnp.float32
bf16 = jnp.bfloat16
AXES = ("gx", "gy", "gz")
NB = 45
NT = 149
R = 8
TAPS = 17

VM = pl.BlockSpec(memory_space=pltpu.VMEM)
SM = pl.BlockSpec(memory_space=pltpu.SMEM)
PARAMS = pltpu.CompilerParams(vmem_limit_bytes=60 * 1024 * 1024)


def shift(value, axis, step):
    count = lax.axis_size(axis)
    return lax.ppermute(value, axis, [(i, (i + step) % count) for i in range(count)])


def split(a):
    hi = a.astype(bf16)
    lo = (a - hi.astype(f32)).astype(bf16)
    return hi, lo


def mm(a, b):
    return jnp.dot(a, b, preferred_element_type=f32)


def iota(shape, dim):
    return lax.broadcasted_iota(jnp.int32, shape, dim)


def banded(taps, base, delta):
    out = jnp.zeros(delta.shape, f32)
    for k in range(TAPS):
        out = jnp.where(delta == k, taps[base + k], out)
    return out


def tap_base(t, axis):
    return (t * 3 + axis) * TAPS


def x_weights(taps, coarse):
    sh = 1 if coarse else 0
    scale = 0.125 if coarse else 1.0
    edge = 128 >> sh

    def halves(rows, source):
        cols = iota((rows, 128), 1) >> sh
        return jnp.concatenate(
            [banded(taps, tap_base(t, 0), source - cols + R) * scale for t in range(2)], axis=1
        )

    hi, lo = split(halves(128, iota((128, 128), 0) >> sh))
    h = iota((16, 128), 0)
    hhi, hlo = split(halves(16, jnp.where(h < 8, h - 8, h - 8 + edge)))
    return (
        jnp.concatenate([hi, hi], axis=0),
        lo,
        jnp.concatenate([hhi, hhi, hlo], axis=0),
    )


def y_weights(taps, t, coarse):
    seg = 48 if coarse else 80
    c = iota((64, 256), 1)
    i = iota((64, 256), 0) >> (1 if coarse else 0)
    j = c - jnp.where(c >= seg, seg, 0) - jnp.where(c >= 2 * seg, seg, 0)
    m = jnp.where(c < 3 * seg, banded(taps, tap_base(t, 1), j - i), 0.0)
    hi = m.astype(bf16).astype(f32)
    return jnp.where(c < 2 * seg, hi, m - hi).astype(bf16)


def stack(hi, lo):
    pad = jnp.zeros((256 - 3 * hi.shape[0], hi.shape[1]), bf16)
    return jnp.concatenate([hi, lo, hi, pad], axis=0)


def x_block(a, xt, w1, w2, wh):
    hi, lo = split(a)
    xhi, xlo = split(xt)
    x3 = jnp.concatenate([xhi, xlo, xhi], axis=0)
    return (
        mm(jnp.concatenate([hi, lo], axis=1), w1)
        + mm(hi, w2)
        + lax.dot_general(x3, wh, (((0,), (0,)), ((), ())), preferred_element_type=f32)
    )


def pool(ref, z):
    def half(p):
        return ref[p, pl.ds(0, 128, stride=2), :] + ref[p, pl.ds(1, 128, stride=2), :]

    return half(2 * z) + half(2 * z + 1)


def prep_kernel(d, g, ylo, yhi):
    def step(z, acc):
        v = pool(d, z)
        g[z] = v
        return acc + v

    total = lax.fori_loop(0, 16, step, jnp.zeros((128, 128), f32))
    rows = jnp.sum(total.reshape(8, 16, 128), axis=1)
    group = jnp.where((iota((128, 128), 0) >> 5) == iota((128, 128), 1), 0.125, 0.0)
    q = jnp.dot(rows, group, precision=lax.Precision.HIGHEST, preferred_element_type=f32)
    ylo[0:32] = d[:, 0:8, :]
    yhi[0:32] = d[:, 248:256, :]
    ylo[32:48] = g[:, 0:8, :]
    yhi[32:48] = g[:, 120:128, :]
    ylo[48] = q
    yhi[48] = q


def strip_kernel(d, g, yl, yh, q2, xlo, xhi):
    h = iota((16, 256), 0)
    x = iota((16, 256), 1) & 127
    sel = jnp.where(x == jnp.where(h < 8, h, h + 112), 1.0, 0.0).astype(bf16)
    selc = jnp.where((x >> 1) == jnp.where(h < 8, h, h + 48), 1.0, 0.0).astype(bf16)

    def put(i, rows, s):
        hi, lo = split(rows)
        v = lax.dot_general(
            s, jnp.concatenate([hi, lo], axis=1), (((1,), (1,)), ((), ())),
            preferred_element_type=f32,
        )
        xlo[i] = v[0:8]
        xhi[i] = v[8:16]

    @pl.loop(0, 32)
    def _(z):
        put(z, d[z], sel)

    put(32, yl[0:32].reshape(256, 128), sel)
    put(33, yh[0:32].reshape(256, 128), sel)

    @pl.loop(0, 8)
    def _(b):
        put(34 + b, g[pl.ds(2 * b, 2)].reshape(256, 128), selc)

    put(
        42,
        jnp.concatenate([yl[32:48].reshape(128, 128), yh[32:48].reshape(128, 128)], axis=0),
        selc,
    )
    mine = xlo.at[43]
    own = jnp.concatenate([yl[48], yh[48]], axis=1)
    rest = jnp.concatenate([q2[0], q2[1]], axis=1)
    mine[...] = own
    xlo[44] = rest
    xhi[43] = own
    xhi[44] = rest


def zstrip_kernel(g, yl, yh, xl, xr, qt, zlo, zhi):
    packed = jnp.concatenate([qt[i][:, 0:4] for i in range(32)], axis=1)
    for out, p0, far in ((zlo, 0, 4), (zhi, 24, 8)):
        for p in range(8):
            for s, src in ((0, xl), (1, xr)):
                for half in range(2):
                    out[p * 4 + s * 2 + half] = src[p0 + p, :, half * 128 : half * 128 + 128]
        out[32:40] = yl[p0 : p0 + 8]
        out[40:48] = yh[p0 : p0 + 8]
        for s, src in ((0, xl), (1, xr)):
            a, b = src[32], src[33]
            out[48 + s] = jnp.concatenate([a[:, p0 * 8 : p0 * 8 + 64], b[:, p0 * 8 : p0 * 8 + 64]], axis=1)
        for i in range(4):
            out[50 + 16 * i : 66 + 16 * i] = g[far + i].reshape(16, 8, 128)
        c0 = 0 if p0 == 0 else 8
        out[114:122] = yl[32 + c0 : 40 + c0]
        out[122:130] = yh[32 + c0 : 40 + c0]
        for b in range(4):
            for s, src in ((0, xl), (1, xr)):
                for half in range(2):
                    out[130 + b * 4 + s * 2 + half] = src[34 + c0 // 2 + b, :, half * 128 : half * 128 + 128]
        for s, src in ((0, xl), (1, xr)):
            a = src[42]
            out[146 + s] = jnp.concatenate(
                [a[:, c0 * 8 : c0 * 8 + 64], a[:, 128 + c0 * 8 : 128 + c0 * 8 + 64]], axis=1
            )
        out[148] = packed


def own_kernel(ft, ct, d, g, yl, yh, xl, xr, e, ec):
    w = x_weights(ft, False)

    def strip(i):
        return jnp.concatenate([xl[i], xr[i]], axis=0)

    @pl.loop(0, 32)
    def _(z):
        r = x_block(d[z], strip(z), *w)
        for t in range(2):
            e[t, z, 8:264, :] = r[:, t * 128 : t * 128 + 128]

    for i, src, row in ((32, yl, 0), (33, yh, 264)):
        r = x_block(src[0:32].reshape(256, 128), strip(i), *w).reshape(32, 8, 256)
        for t in range(2):
            e[t, :, row : row + 8, :] = r[:, :, t * 128 : t * 128 + 128]

    wc = x_weights(ct, True)

    @pl.loop(0, 8)
    def _(b):
        r = x_block(g[pl.ds(2 * b, 2)].reshape(256, 128), strip(34 + b), *wc).reshape(2, 128, 256)
        for t in range(2):
            ec[t, pl.ds(2 * b, 2), 8:136, :] = r[:, :, t * 128 : t * 128 + 128]

    r = x_block(
        jnp.concatenate([yl[32:48].reshape(128, 128), yh[32:48].reshape(128, 128)], axis=0),
        strip(42), *wc,
    ).reshape(2, 16, 8, 256)
    for t in range(2):
        ec[t, :, 0:8, :] = r[0, :, :, t * 128 : t * 128 + 128]
        ec[t, :, 136:144, :] = r[1, :, :, t * 128 : t * 128 + 128]


def z_group(planes, taps, base, count):
    w = [jnp.full((8, 128), taps[base + k], f32) for k in range(TAPS)]
    w = [jnp.concatenate([v, v], axis=0) for v in w]
    acc = [None] * count
    for i in range(count + 2 * R):
        v = planes(i)
        for o in range(count):
            k = i - o
            if 0 <= k < TAPS:
                acc[o] = w[k] * v if acc[o] is None else acc[o] + w[k] * v
    return acc


def final_kernel(ft, ct, e, ec, zl, zh, sl, sh, tp, out, eh, ech, gn, fh, fl, fch, fcl):
    w = x_weights(ft, False)

    def strip(ref, i):
        return jnp.concatenate(
            [
                jnp.concatenate([ref[i], ref[i + 1]], axis=1),
                jnp.concatenate([ref[i + 2], ref[i + 3]], axis=1),
            ],
            axis=0,
        )

    for n, (m, s) in enumerate(((zl, sl), (zh, sh))):

        @pl.loop(0, 8)
        def _(p, n=n, m=m, s=s):
            r = x_block(m[p], strip(s, 4 * p), *w)
            for t in range(2):
                eh[t, 8 * n + p, 8:264, :] = r[:, t * 128 : t * 128 + 128]

        @pl.loop(0, 4)
        def _(p, n=n, m=m):
            gn[4 * n + p] = pool(m, p)

    def sides(lo, hi):
        return jnp.concatenate([lo, hi], axis=0)

    def pair(i):
        return jnp.concatenate(
            [jnp.concatenate([sl[i], sh[i]], axis=1), jnp.concatenate([sl[i + 1], sh[i + 1]], axis=1)],
            axis=0,
        )

    r = x_block(
        sides(sl[32:48].reshape(128, 128), sh[32:48].reshape(128, 128)), pair(48), *w
    ).reshape(2, 2, 8, 8, 256)
    for n in range(2):
        for t in range(2):
            eh[t, 8 * n : 8 * n + 8, 0:8, :] = r[n, 0, :, :, t * 128 : t * 128 + 128]
            eh[t, 8 * n : 8 * n + 8, 264:272, :] = r[n, 1, :, :, t * 128 : t * 128 + 128]

    wc = x_weights(ct, True)
    for n, s in enumerate((sl, sh)):
        for b in range(4):
            near = b >= 2 if n == 0 else b < 2
            if near:
                first = 2 * (b - 2) if n == 0 else 4 + 2 * b
                rows = gn[first : first + 2].reshape(256, 128)
            else:
                first = 50 + 32 * (b if n == 0 else b - 2)
                rows = s[first : first + 32].reshape(256, 128)
            r = x_block(rows, strip(s, 130 + 4 * b), *wc).reshape(2, 128, 256)
            for t in range(2):
                ech[t, 8 * n + 2 * b : 8 * n + 2 * b + 2, 8:136, :] = r[:, :, t * 128 : t * 128 + 128]
    r = x_block(
        sides(sl[114:130].reshape(128, 128), sh[114:130].reshape(128, 128)), pair(146), *wc
    ).reshape(2, 2, 8, 8, 256)
    for n in range(2):
        for t in range(2):
            ech[t, 8 * n : 8 * n + 8, 0:8, :] = r[n, 0, :, :, t * 128 : t * 128 + 128]
            ech[t, 8 * n : 8 * n + 8, 136:144, :] = r[n, 1, :, :, t * 128 : t * 128 + 128]

    @pl.loop(0, 17)
    def _(y):
        rows = pl.ds(pl.multiple_of(y * 16, 16), 16)
        for t in range(2):
            for zb in range(4):

                def plane(i, t=t, zb=zb):
                    i = i + 8 * zb
                    if i < 8:
                        return eh[t, i, rows, :]
                    if i < 40:
                        return e[t, i - 8, rows, :]
                    return eh[t, i - 32, rows, :]

                for o, v in enumerate(z_group(plane, ft, tap_base(t, 2), 8)):
                    z = 8 * zb + o
                    q, l, r = z // 4, z // 2 % 2, z % 2
                    hi, lo = split(v)
                    fh[t, 2 * q + r, rows, l * 128 : l * 128 + 128] = hi
                    fl[t, 2 * q + r, rows, l * 128 : l * 128 + 128] = lo

    @pl.loop(0, 9)
    def _(y):
        rows = pl.ds(pl.multiple_of(y * 16, 16), 16)
        for t in range(2):
            for zb in range(2):

                def plane(i, t=t, zb=zb):
                    i = i + 8 * zb
                    if i < 8:
                        return ech[t, i, rows, :]
                    if i < 24:
                        return ec[t, i - 8, rows, :]
                    return ech[t, i - 16, rows, :]

                for o, v in enumerate(z_group(plane, ct, tap_base(t, 2), 8)):
                    z = 8 * zb + o
                    hi, lo = split(v)
                    fch[t, z // 2, rows, (z % 2) * 128 : (z % 2) * 128 + 128] = hi
                    fcl[t, z // 2, rows, (z % 2) * 128 : (z % 2) * 128 + 128] = lo

    wy, wyc = (
        jnp.concatenate([y_weights(taps, t, coarse) for t in range(2)], axis=1)
        for taps, coarse in ((ft, False), (ct, True))
    )

    def stacked(h, l, index, first, size):
        rows = slice(first, first + size)
        return jnp.concatenate([stack(h[t, index, rows, :], l[t, index, rows, :]) for t in range(2)], axis=0)

    @pl.loop(0, 8)
    def _(q):
        for b in range(4):
            top = jnp.concatenate(
                [jnp.broadcast_to(tp[2 * b + k : 2 * b + k + 1, :], (32, 128)) for k in range(2)], axis=0
            )
            common = mm(wyc, stacked(fch, fcl, q, 32 * b, 48))
            even, odd = common[:, 0:128] + top, common[:, 128:256] + top
            for r in range(2):
                res = mm(wy, stacked(fh, fl, 2 * q + r, 64 * b, 80))
                out[4 * q + r, 64 * b : 64 * b + 64, :] = res[:, 0:128] + even
                out[4 * q + 2 + r, 64 * b : 64 * b + 64, :] = res[:, 128:256] + odd


def sds(*shape):
    return jax.ShapeDtypeStruct(shape, f32)


def call(kernel, outs, n_smem, args, scratch=(), flops=0, nbytes=0):
    return pl.pallas_call(
        kernel,
        out_shape=outs,
        in_specs=[SM] * n_smem + [VM] * (len(args) - n_smem),
        out_specs=jax.tree.map(lambda _: VM, outs),
        scratch_shapes=scratch,
        compiler_params=PARAMS,
        cost_estimate=pl.CostEstimate(flops=flops, bytes_accessed=nbytes, transcendentals=0),
    )(*args)


OFFSETS = {"gx": (0, -1, 1, -4, -3, -2, 2, 3), "gy": (0, -1, 1, 2), "gz": (0, -1, 1, -4, -3, -2, 2, 3)}


def wrapped(d, period):
    d = jnp.abs(d) % period
    return jnp.minimum(d, period - d).astype(f32)


def top_kernel_matrix():
    shape = (8, 4, 8, 8, 8, 4, 4)
    ids = [lax.broadcasted_iota(jnp.int32, shape, i) for i in range(7)]
    return ids


def top_potential(parts):
    lane = jnp.arange(128, dtype=jnp.int32)
    offx = sum(jnp.where(lane // 16 == i, v, 0) for i, v in enumerate(OFFSETS["gx"]))
    offy = sum(jnp.where(lane // 4 % 4 == i, v, 0) for i, v in enumerate(OFFSETS["gy"]))
    zi = jnp.arange(8, dtype=jnp.int32)
    dz = wrapped(sum(jnp.where(zi == i, v, 0) for i, v in enumerate(OFFSETS["gz"])), 8)
    ys = offy[None, :] * 8 + jnp.arange(8, dtype=jnp.int32)[:, None]
    xs = offx * 4 + lane % 4
    own = jnp.arange(32, dtype=jnp.int32)
    dy = wrapped((own // 4)[:, None, None] - ys[None], 32)
    dx = wrapped((own % 4)[:, None, None] - xs[None, None, :], 32)
    r2 = 1.0 + (dz * dz)[None, :, None, None] + (dy * dy + dx * dx)[:, None]
    kernel = 1.0 / (256.0 * jnp.sqrt(r2))
    return jnp.sum(kernel * parts[None], axis=(1, 2, 3)).reshape(8, 4)


def on_device(charges, fine_taps, coarse_taps):
    ft = fine_taps.reshape(-1)
    ct = coarse_taps.reshape(-1)
    zl = shift(charges[24:32], "gz", 1)
    zh = shift(charges[0:8], "gz", -1)

    g, ylo, yhi = call(
        prep_kernel, (sds(16, 128, 128), sds(49, 8, 128), sds(49, 8, 128)), 0, (charges,),
        flops=1 << 22, nbytes=6 << 20,
    )
    q2 = shift(ylo[48], "gy", 2)
    yl = shift(yhi, "gy", 1)
    yh = shift(ylo, "gy", -1)
    q2 = jnp.stack([ylo[48], q2])

    xlo, xhi = call(
        strip_kernel, (sds(NB, 8, 256), sds(NB, 8, 256)), 0, (charges, g, yl, yh, q2),
        flops=1 << 27, nbytes=6 << 20,
    )
    xl = shift(xhi, "gx", 1)
    xr = shift(xlo, "gx", -1)

    def quarters(v):
        v = v[43:45]
        return jnp.stack([v[1, :, 0:128], v[0, :, 0:128], v[0, :, 128:256], v[1, :, 128:256]])

    q3 = jnp.concatenate([quarters(v) for v in (xlo, xl, xr)], axis=0)
    qm = shift(q3, "gx", 3)
    qp = shift(q3, "gx", -3)
    qt = jnp.concatenate([q3, qm[4:8], qm[0:4], qm[8:12], qp[4:8], qp[0:4]], axis=0)

    zlo, zhi = call(
        zstrip_kernel, (sds(NT, 8, 128), sds(NT, 8, 128)), 0, (g, yl, yh, xl, xr, qt),
        flops=1 << 20, nbytes=4 << 20,
    )
    sl = shift(zhi, "gz", 1)
    sh = shift(zlo, "gz", -1)

    e, ec = call(
        own_kernel, (sds(2, 32, 272, 128), sds(2, 16, 144, 128)), 2,
        (ft, ct, charges, g, yl, yh, xl, xr), flops=5 << 30, nbytes=16 << 20,
    )

    p3 = jnp.stack([zlo[148], sl[148], sh[148]])
    pm = shift(p3, "gz", 3)
    pp = shift(p3, "gz", -3)
    parts = jnp.stack([p3[0], p3[1], p3[2], pm[1], pm[0], pm[2], pp[1], pp[0]])
    tp = jnp.repeat(top_potential(parts), 32, axis=1)

    return call(
        final_kernel, sds(32, 256, 128), 2, (ft, ct, e, ec, zl, zh, sl, sh, tp),
        scratch=[
            pltpu.VMEM((2, 16, 272, 128), f32),
            pltpu.VMEM((2, 16, 144, 128), f32),
            pltpu.VMEM((8, 128, 128), f32),
            pltpu.VMEM((2, 16, 272, 256), bf16),
            pltpu.VMEM((2, 16, 272, 256), bf16),
            pltpu.VMEM((2, 8, 144, 256), bf16),
            pltpu.VMEM((2, 8, 144, 256), bf16),
        ],
        flops=8 << 30, nbytes=20 << 20,
    )


def solution(mesh):
    return jax.shard_map(
        on_device,
        mesh=mesh,
        in_specs=(P("gz", "gy", "gx"), P(), P()),
        out_specs=P("gz", "gy", "gx"),
        check_vma=False,
    )
```

```python
import jax
import jax.numpy as jnp
from jax import lax
from jax.experimental import pallas as pl
from jax.experimental.pallas import tpu as pltpu
from jax.sharding import PartitionSpec as P


f32 = jnp.float32
bf16 = jnp.bfloat16
NB = 45
NT = 148
R = 8
TAPS = 17

VM = pl.BlockSpec(memory_space=pltpu.VMEM)
SM = pl.BlockSpec(memory_space=pltpu.SMEM)
PARAMS = pltpu.CompilerParams(vmem_limit_bytes=60 * 1024 * 1024)


def shift(value, axis, step):
    count = lax.axis_size(axis)
    return lax.ppermute(value, axis, [(i, (i + step) % count) for i in range(count)])


def split(a):
    hi = a.astype(bf16)
    lo = (a - hi.astype(f32)).astype(bf16)
    return hi, lo


def mm(a, b):
    return jnp.dot(a, b, preferred_element_type=f32)


def iota(shape, dim):
    return lax.broadcasted_iota(jnp.int32, shape, dim)


def banded(taps, base, delta):
    out = jnp.zeros(delta.shape, f32)
    for k in range(TAPS):
        out = jnp.where(delta == k, taps[base + k], out)
    return out


def tap_base(t, axis):
    return (t * 3 + axis) * TAPS


def x_weights(taps, coarse):
    sh = 1 if coarse else 0
    scale = 0.125 if coarse else 1.0
    edge = 128 >> sh

    def halves(rows, source):
        cols = iota((rows, 128), 1) >> sh
        return jnp.concatenate(
            [banded(taps, tap_base(t, 0), source - cols + R) * scale for t in range(2)], axis=1
        )

    hi, lo = split(halves(128, iota((128, 128), 0) >> sh))
    h = iota((16, 128), 0)
    hhi, hlo = split(halves(16, jnp.where(h < 8, h - 8, h - 8 + edge)))
    return jnp.concatenate([hi, hi, lo, hhi, hhi, hlo, jnp.zeros((80, 256), bf16)], axis=0)


def y_weights(taps, t, coarse):
    seg = 48 if coarse else 80
    c = iota((64, 256), 1)
    i = iota((64, 256), 0) >> (1 if coarse else 0)
    j = c - jnp.where(c >= seg, seg, 0) - jnp.where(c >= 2 * seg, seg, 0)
    m = jnp.where(c < 3 * seg, banded(taps, tap_base(t, 1), j - i), 0.0)
    hi = m.astype(bf16).astype(f32)
    return jnp.where(c < 2 * seg, hi, m - hi).astype(bf16)


def stack(hi, lo):
    pad = jnp.zeros((256 - 3 * hi.shape[0], hi.shape[1]), bf16)
    return jnp.concatenate([hi, lo, hi, pad], axis=0)


def x_block(a, xt, w):
    hi, lo = split(a)
    xhi, xlo = split(xt)
    x3 = jnp.concatenate([xhi, xlo, xhi, jnp.zeros((80, 256), bf16)], axis=0)
    return mm(jnp.concatenate([hi, lo, hi, x3.T], axis=1), w)


def pool(ref, z):
    def half(p):
        return ref[p, pl.ds(0, 128, stride=2), :] + ref[p, pl.ds(1, 128, stride=2), :]

    return half(2 * z) + half(2 * z + 1)


def prep_kernel(d, g, ylo, yhi):
    def step(z, acc):
        v = pool(d, z)
        g[z] = v
        return acc + v

    total = lax.fori_loop(0, 16, step, jnp.zeros((128, 128), f32))
    rows = jnp.sum(total.reshape(8, 16, 128), axis=1)
    group = jnp.where((iota((128, 128), 0) >> 5) == iota((128, 128), 1), 0.125, 0.0)
    q = jnp.dot(rows, group, precision=lax.Precision.HIGHEST, preferred_element_type=f32)
    ylo[0:32] = d[:, 0:8, :]
    yhi[0:32] = d[:, 248:256, :]
    ylo[32:48] = g[:, 0:8, :]
    yhi[32:48] = g[:, 120:128, :]
    ylo[48] = q
    yhi[48] = q


def strip_kernel(d, g, yl, yh, q2, xlo, xhi):
    lane = iota((256, 128), 1)

    def put(first, sources):
        tile = None
        for p, v in enumerate(sources):
            v = pltpu.roll(v, (16 * p + 8) % 128, 1)
            tile = v if tile is None else jnp.where(lane >= 16 * p, v, tile)
        tile = tile.T
        for p in range(len(sources)):
            xhi[first + p] = tile[16 * p : 16 * p + 8]
            xlo[first + p] = tile[16 * p + 8 : 16 * p + 16]

    for k in range(4):
        put(8 * k, [d[8 * k + p] for p in range(8)])
    put(32, [yl[0:32].reshape(256, 128), yh[0:32].reshape(256, 128)])

    def putc(first, sources):
        tile = None
        for p, v in enumerate(sources):
            v = v + pltpu.roll(v, 127, 1)
            v = pltpu.roll(v, (32 * p + 16) % 128, 1)
            tile = v if tile is None else jnp.where(lane >= 32 * p, v, tile)
        tile = tile.T
        for p in range(len(sources)):
            rows = [tile[32 * p + 2 * i : 32 * p + 2 * i + 1] for i in range(16)]
            xhi[first + p] = jnp.concatenate(rows[0:8], axis=0)
            xlo[first + p] = jnp.concatenate(rows[8:16], axis=0)

    for k in range(2):
        putc(34 + 4 * k, [g[8 * k + 2 * p : 8 * k + 2 * p + 2].reshape(256, 128) for p in range(4)])
    putc(
        42,
        [jnp.concatenate([yl[32:48].reshape(128, 128), yh[32:48].reshape(128, 128)], axis=0)],
    )
    own = jnp.concatenate([yl[48], yh[48]], axis=1)
    rest = jnp.concatenate([q2[0], q2[1]], axis=1)
    xlo[43] = own
    xlo[44] = rest
    xhi[43] = own
    xhi[44] = rest


def zstrip_kernel(g, yl, yh, xl, xr, own, zlo, zhi, q3):
    for i, src in enumerate((own, xl, xr)):
        a, b = src[43], src[44]
        q3[4 * i] = b[:, 0:128]
        q3[4 * i + 1] = a[:, 0:128]
        q3[4 * i + 2] = a[:, 128:256]
        q3[4 * i + 3] = b[:, 128:256]
    for out, p0, far in ((zlo, 0, 4), (zhi, 24, 8)):
        for p in range(8):
            for s, src in ((0, xl), (1, xr)):
                for half in range(2):
                    out[p * 4 + s * 2 + half] = src[p0 + p, :, half * 128 : half * 128 + 128]
        out[32:40] = yl[p0 : p0 + 8]
        out[40:48] = yh[p0 : p0 + 8]
        for s, src in ((0, xl), (1, xr)):
            a, b = src[32], src[33]
            out[48 + s] = jnp.concatenate([a[:, p0 * 8 : p0 * 8 + 64], b[:, p0 * 8 : p0 * 8 + 64]], axis=1)
        for i in range(4):
            out[50 + 16 * i : 66 + 16 * i] = g[far + i].reshape(16, 8, 128)
        c0 = 0 if p0 == 0 else 8
        out[114:122] = yl[32 + c0 : 40 + c0]
        out[122:130] = yh[32 + c0 : 40 + c0]
        for b in range(4):
            for s, src in ((0, xl), (1, xr)):
                for half in range(2):
                    out[130 + b * 4 + s * 2 + half] = src[34 + c0 // 2 + b, :, half * 128 : half * 128 + 128]
        for s, src in ((0, xl), (1, xr)):
            a = src[42]
            out[146 + s] = jnp.concatenate(
                [a[:, c0 * 8 : c0 * 8 + 64], a[:, 128 + c0 * 8 : 128 + c0 * 8 + 64]], axis=1
            )


def pack_kernel(q3, qm, qp, packed):
    tiles = [q3[i] for i in range(12)]
    tiles += [qm[i] for i in (4, 5, 6, 7, 0, 1, 2, 3, 8, 9, 10, 11)]
    tiles += [qp[i] for i in (4, 5, 6, 7, 0, 1, 2, 3)]
    packed[...] = jnp.concatenate([v[:, 0:4] for v in tiles], axis=1)


def own_fine_kernel(ft, d, yl, yh, xl, xr, e):
    w = x_weights(ft, False)

    def strip(i):
        return jnp.concatenate([xl[i], xr[i]], axis=0)

    @pl.loop(0, 32, unroll=4)
    def _(z):
        r = x_block(d[z], strip(z), w)
        for t in range(2):
            e[t, z, 8:264, :] = r[:, t * 128 : t * 128 + 128]

    for i, src, row in ((32, yl, 0), (33, yh, 264)):
        r = x_block(src[0:32].reshape(256, 128), strip(i), w).reshape(32, 8, 256)
        for t in range(2):
            e[t, :, row : row + 8, :] = r[:, :, t * 128 : t * 128 + 128]


def own_coarse_kernel(ct, g, yl, yh, xl, xr, ec):
    def strip(i):
        return jnp.concatenate([xl[i], xr[i]], axis=0)

    wc = x_weights(ct, True)

    @pl.loop(0, 8, unroll=4)
    def _(b):
        r = x_block(g[pl.ds(2 * b, 2)].reshape(256, 128), strip(34 + b), wc).reshape(2, 128, 256)
        for t in range(2):
            ec[t, pl.ds(2 * b, 2), 8:136, :] = r[:, :, t * 128 : t * 128 + 128]

    r = x_block(
        jnp.concatenate([yl[32:48].reshape(128, 128), yh[32:48].reshape(128, 128)], axis=0),
        strip(42), wc,
    ).reshape(2, 16, 8, 256)
    for t in range(2):
        ec[t, :, 0:8, :] = r[0, :, :, t * 128 : t * 128 + 128]
        ec[t, :, 136:144, :] = r[1, :, :, t * 128 : t * 128 + 128]


def z_group(planes, taps, base, count):
    w = [jnp.full((8, 128), taps[base + k], f32) for k in range(TAPS)]
    w = [jnp.concatenate([v, v], axis=0) for v in w]
    acc = [None] * count
    for i in range(count + 2 * R):
        v = planes(i)
        for o in range(count):
            k = i - o
            if 0 <= k < TAPS:
                acc[o] = w[k] * v if acc[o] is None else acc[o] + w[k] * v
    return acc


def final_kernel(ft, ct, e, ec, zl, zh, sl, sh, out, eh, ech, gn, fh, fl, fch, fcl):
    w = x_weights(ft, False)

    def strip(ref, i):
        return jnp.concatenate(
            [
                jnp.concatenate([ref[i], ref[i + 1]], axis=1),
                jnp.concatenate([ref[i + 2], ref[i + 3]], axis=1),
            ],
            axis=0,
        )

    for n, (m, s) in enumerate(((zl, sl), (zh, sh))):

        @pl.loop(0, 8, unroll=4)
        def _(p, n=n, m=m, s=s):
            r = x_block(m[p], strip(s, 4 * p), w)
            for t in range(2):
                eh[t, 8 * n + p, 8:264, :] = r[:, t * 128 : t * 128 + 128]

        @pl.loop(0, 4)
        def _(p, n=n, m=m):
            gn[4 * n + p] = pool(m, p)

    def sides(lo, hi):
        return jnp.concatenate([lo, hi], axis=0)

    def pair(i):
        return jnp.concatenate(
            [jnp.concatenate([sl[i], sh[i]], axis=1), jnp.concatenate([sl[i + 1], sh[i + 1]], axis=1)],
            axis=0,
        )

    r = x_block(
        sides(sl[32:48].reshape(128, 128), sh[32:48].reshape(128, 128)), pair(48), w
    ).reshape(2, 2, 8, 8, 256)
    for n in range(2):
        for t in range(2):
            eh[t, 8 * n : 8 * n + 8, 0:8, :] = r[n, 0, :, :, t * 128 : t * 128 + 128]
            eh[t, 8 * n : 8 * n + 8, 264:272, :] = r[n, 1, :, :, t * 128 : t * 128 + 128]

    wc = x_weights(ct, True)
    for n, s in enumerate((sl, sh)):
        for b in range(4):
            near = b >= 2 if n == 0 else b < 2
            if near:
                first = 2 * (b - 2) if n == 0 else 4 + 2 * b
                rows = gn[first : first + 2].reshape(256, 128)
            else:
                first = 50 + 32 * (b if n == 0 else b - 2)
                rows = s[first : first + 32].reshape(256, 128)
            r = x_block(rows, strip(s, 130 + 4 * b), wc).reshape(2, 128, 256)
            for t in range(2):
                ech[t, 8 * n + 2 * b : 8 * n + 2 * b + 2, 8:136, :] = r[:, :, t * 128 : t * 128 + 128]
    r = x_block(
        sides(sl[114:130].reshape(128, 128), sh[114:130].reshape(128, 128)), pair(146), wc
    ).reshape(2, 2, 8, 8, 256)
    for n in range(2):
        for t in range(2):
            ech[t, 8 * n : 8 * n + 8, 0:8, :] = r[n, 0, :, :, t * 128 : t * 128 + 128]
            ech[t, 8 * n : 8 * n + 8, 136:144, :] = r[n, 1, :, :, t * 128 : t * 128 + 128]

    @pl.loop(0, 17)
    def _(y):
        rows = pl.ds(pl.multiple_of(y * 16, 16), 16)
        for t in range(2):
            for zb in range(4):

                def plane(i, t=t, zb=zb):
                    i = i + 8 * zb
                    if i < 8:
                        return eh[t, i, rows, :]
                    if i < 40:
                        return e[t, i - 8, rows, :]
                    return eh[t, i - 32, rows, :]

                for o, v in enumerate(z_group(plane, ft, tap_base(t, 2), 8)):
                    z = 8 * zb + o
                    q, l, r = z // 4, z // 2 % 2, z % 2
                    hi, lo = split(v)
                    fh[t, 2 * q + r, rows, l * 128 : l * 128 + 128] = hi
                    fl[t, 2 * q + r, rows, l * 128 : l * 128 + 128] = lo

    @pl.loop(0, 9)
    def _(y):
        rows = pl.ds(pl.multiple_of(y * 16, 16), 16)
        for t in range(2):
            for zb in range(2):

                def plane(i, t=t, zb=zb):
                    i = i + 8 * zb
                    if i < 8:
                        return ech[t, i, rows, :]
                    if i < 24:
                        return ec[t, i - 8, rows, :]
                    return ech[t, i - 16, rows, :]

                for o, v in enumerate(z_group(plane, ct, tap_base(t, 2), 8)):
                    z = 8 * zb + o
                    hi, lo = split(v)
                    fch[t, z // 2, rows, (z % 2) * 128 : (z % 2) * 128 + 128] = hi
                    fcl[t, z // 2, rows, (z % 2) * 128 : (z % 2) * 128 + 128] = lo

    wy, wyc = (
        jnp.concatenate([y_weights(taps, t, coarse) for t in range(2)], axis=1)
        for taps, coarse in ((ft, False), (ct, True))
    )

    def stacked(h, l, index, first, size):
        rows = slice(first, first + size)
        return jnp.concatenate([stack(h[t, index, rows, :], l[t, index, rows, :]) for t in range(2)], axis=0)

    @pl.loop(0, 8)
    def _(q):
        for b in range(4):
            common = mm(wyc, stacked(fch, fcl, q, 32 * b, 48))
            even, odd = common[:, 0:128], common[:, 128:256]
            for r in range(2):
                res = mm(wy, stacked(fh, fl, 2 * q + r, 64 * b, 80))
                out[4 * q + r, 64 * b : 64 * b + 64, :] = res[:, 0:128] + even
                out[4 * q + 2 + r, 64 * b : 64 * b + 64, :] = res[:, 128:256] + odd


def sds(*shape):
    return jax.ShapeDtypeStruct(shape, f32)


def call(kernel, outs, n_smem, args, scratch=(), flops=0, nbytes=0):
    return pl.pallas_call(
        kernel,
        out_shape=outs,
        in_specs=[SM] * n_smem + [VM] * (len(args) - n_smem),
        out_specs=jax.tree.map(lambda _: VM, outs),
        scratch_shapes=scratch,
        compiler_params=PARAMS,
        cost_estimate=pl.CostEstimate(flops=flops, bytes_accessed=nbytes, transcendentals=0),
    )(*args)


OFFSETS = {"gx": (0, -1, 1, -4, -3, -2, 2, 3), "gy": (0, -1, 1, 2), "gz": (0, -1, 1, -4, -3, -2, 2, 3)}


def wrapped(d, period):
    d = jnp.abs(d) % period
    return jnp.minimum(d, period - d).astype(f32)


def top_potential(parts):
    lane = jnp.arange(128, dtype=jnp.int32)
    offx = sum(jnp.where(lane // 16 == i, v, 0) for i, v in enumerate(OFFSETS["gx"]))
    offy = sum(jnp.where(lane // 4 % 4 == i, v, 0) for i, v in enumerate(OFFSETS["gy"]))
    zi = jnp.arange(8, dtype=jnp.int32)
    dz = wrapped(sum(jnp.where(zi == i, v, 0) for i, v in enumerate(OFFSETS["gz"])), 8)
    ys = offy[None, :] * 8 + jnp.arange(8, dtype=jnp.int32)[:, None]
    xs = offx * 4 + lane % 4
    own = jnp.arange(32, dtype=jnp.int32)
    dy = wrapped((own // 4)[:, None, None] - ys[None], 32)
    dx = wrapped((own % 4)[:, None, None] - xs[None, None, :], 32)
    r2 = 1.0 + (dz * dz)[None, :, None, None] + (dy * dy + dx * dx)[:, None]
    kernel = 1.0 / (256.0 * jnp.sqrt(r2))
    return jnp.sum(kernel * parts[None], axis=(1, 2, 3)).reshape(8, 4)


def body(charges, fine_taps, coarse_taps):
    ft = fine_taps.reshape(-1)
    ct = coarse_taps.reshape(-1)
    zl = shift(charges[24:32], "gz", 1)
    zh = shift(charges[0:8], "gz", -1)

    g, ylo, yhi = call(
        prep_kernel, (sds(16, 128, 128), sds(49, 8, 128), sds(49, 8, 128)), 0, (charges,),
        flops=1 << 22, nbytes=6 << 20,
    )
    q2 = shift(ylo[48], "gy", 2)
    yl = shift(yhi, "gy", 1)
    yh = shift(ylo, "gy", -1)
    q2 = jnp.stack([ylo[48], q2])

    xlo, xhi = call(
        strip_kernel, (sds(NB, 8, 256), sds(NB, 8, 256)), 0, (charges, g, yl, yh, q2),
        flops=1 << 27, nbytes=6 << 20,
    )
    xl = shift(xhi, "gx", 1)
    xr = shift(xlo, "gx", -1)

    zlo, zhi, q3 = call(
        zstrip_kernel, (sds(NT, 8, 128), sds(NT, 8, 128), sds(12, 8, 128)), 0,
        (g, yl, yh, xl, xr, xlo), flops=1 << 20, nbytes=4 << 20,
    )
    sl = shift(zhi, "gz", 1)
    sh = shift(zlo, "gz", -1)
    qm = shift(q3, "gx", 3)
    qp = shift(q3, "gx", -3)

    e = call(
        own_fine_kernel, sds(2, 32, 272, 128), 1,
        (ft, charges, yl, yh, xl, xr), flops=5 << 30, nbytes=16 << 20,
    )

    qm, qp, e = lax.optimization_barrier((qm, qp, e))
    p0 = call(pack_kernel, sds(8, 128), 0, (q3, qm, qp))
    pl1 = shift(p0, "gz", 1)
    pr1 = shift(p0, "gz", -1)
    p0, g = lax.optimization_barrier((p0, g))
    ec = call(
        own_coarse_kernel, sds(2, 16, 144, 128), 1,
        (ct, g, yl, yh, xl, xr), flops=1 << 30, nbytes=4 << 20,
    )
    p3, ec = lax.optimization_barrier((jnp.stack([p0, pl1, pr1]), ec))
    pm = shift(p3, "gz", 3)
    pp = shift(p3, "gz", -3)

    out = call(
        final_kernel, sds(32, 256, 128), 2, (ft, ct, e, ec, zl, zh, sl, sh),
        scratch=[
            pltpu.VMEM((2, 16, 272, 128), f32),
            pltpu.VMEM((2, 16, 144, 128), f32),
            pltpu.VMEM((8, 128, 128), f32),
            pltpu.VMEM((2, 16, 272, 256), bf16),
            pltpu.VMEM((2, 16, 272, 256), bf16),
            pltpu.VMEM((2, 8, 144, 256), bf16),
            pltpu.VMEM((2, 8, 144, 256), bf16),
        ],
        flops=8 << 30, nbytes=20 << 20,
    )
    pm, pp, out = lax.optimization_barrier((pm, pp, out))
    parts = jnp.stack([p3[0], p3[1], p3[2], pm[1], pm[0], pm[2], pp[1], pp[0]])
    tp = jnp.repeat(top_potential(parts), 32, axis=1)
    return (out.reshape(32, 8, 32, 128) + tp[None, :, None, :]).reshape(32, 256, 128)


def solution(mesh):
    return jax.shard_map(
        body,
        mesh=mesh,
        in_specs=(P("gz", "gy", "gx"), P(), P()),
        out_specs=P("gz", "gy", "gx"),
        check_vma=False,
    )
```

```python
import jax
import jax.numpy as jnp
from jax import lax
from jax.experimental import pallas as pl
from jax.experimental.pallas import tpu as pltpu
from jax.sharding import PartitionSpec as P


f32 = jnp.float32
bf16 = jnp.bfloat16
NB = 45
NT = 149
R = 8
TAPS = 17

VM = pl.BlockSpec(memory_space=pltpu.VMEM)
SM = pl.BlockSpec(memory_space=pltpu.SMEM)


def shift(value, axis, step):
    count = lax.axis_size(axis)
    return lax.ppermute(value, axis, [(i, (i + step) % count) for i in range(count)])


def split(a):
    hi = a.astype(bf16)
    lo = (a - hi.astype(f32)).astype(bf16)
    return hi, lo


def mm(a, b):
    return jnp.dot(a, b, preferred_element_type=f32)


def iota(shape, dim):
    return lax.broadcasted_iota(jnp.int32, shape, dim)


def banded(taps, t, axis, delta):
    out = jnp.zeros(delta.shape, f32)
    for k in range(TAPS):
        out = jnp.where(delta == k, taps[t, axis, k], out)
    return out


def x_weights(taps, coarse):
    sh = 1 if coarse else 0
    scale = 0.125 if coarse else 1.0
    edge = 128 >> sh

    def halves(rows, source):
        cols = iota((rows, 128), 1) >> sh
        return jnp.concatenate(
            [banded(taps, t, 0, source - cols + R) * scale for t in range(2)], axis=1
        )

    hi, lo = split(halves(128, iota((128, 128), 0) >> sh))
    h = iota((16, 128), 0)
    hhi, hlo = split(halves(16, jnp.where(h < 8, h - 8, h - 8 + edge)))
    return jnp.concatenate([hi, hi, lo, hhi, hhi, hlo, jnp.zeros((80, 256), bf16)], axis=0)


def y_weights(taps, t, coarse):
    seg = 48 if coarse else 80
    c = iota((64, 256), 1)
    i = iota((64, 256), 0) >> (1 if coarse else 0)
    j = c - jnp.where(c >= seg, seg, 0) - jnp.where(c >= 2 * seg, seg, 0)
    m = jnp.where(c < 3 * seg, banded(taps, t, 1, j - i), 0.0)
    hi = m.astype(bf16).astype(f32)
    return jnp.where(c < 2 * seg, hi, m - hi).astype(bf16)


def stack(hi, lo):
    pad = jnp.zeros((256 - 3 * hi.shape[0], hi.shape[1]), bf16)
    return jnp.concatenate([hi, lo, hi, pad], axis=0)


def x_block(a, xt, w):
    hi, lo = split(a)
    xhi, xlo = split(xt)
    x3 = jnp.concatenate([xhi, xlo, xhi, jnp.zeros((80, 256), bf16)], axis=0)
    return mm(jnp.concatenate([hi, lo, hi, x3.T], axis=1), w)


def pool(ref, z):
    def half(p):
        return ref[p, pl.ds(0, 128, stride=2), :] + ref[p, pl.ds(1, 128, stride=2), :]

    return half(2 * z) + half(2 * z + 1)


def prep_kernel(d, g, ylo, yhi, own):
    def step(z, acc):
        v = pool(d, z)
        g[z] = v
        return acc + v

    total = lax.fori_loop(0, 16, step, jnp.zeros((128, 128), f32))
    rows = jnp.sum(total.reshape(8, 16, 128), axis=1)
    group = jnp.where((iota((128, 128), 0) >> 5) == iota((128, 128), 1), 0.125, 0.0)
    q = jnp.dot(rows, group, precision=lax.Precision.HIGHEST, preferred_element_type=f32)
    ylo[0:32] = d[:, 0:8, :]
    yhi[0:32] = d[:, 248:256, :]
    ylo[32:48] = g[:, 0:8, :]
    yhi[32:48] = g[:, 120:128, :]
    ylo[48] = q
    yhi[48] = q
    own[...] = q


def put(xlo, xhi, first, sources, coarse):
    width = 32 if coarse else 16
    lane = iota((256, 128), 1)
    tile = None
    for p, v in enumerate(sources):
        if coarse:
            v = v + pltpu.roll(v, 127, 1)
        v = pltpu.roll(v, (width * p + width // 2) % 128, 1)
        tile = v if tile is None else jnp.where(lane >= width * p, v, tile)
    tile = tile.T
    for p in range(len(sources)):
        if coarse:
            rows = [tile[32 * p + 2 * i : 32 * p + 2 * i + 1] for i in range(16)]
            xhi[first + p] = jnp.concatenate(rows[0:8], axis=0)
            xlo[first + p] = jnp.concatenate(rows[8:16], axis=0)
        else:
            xhi[first + p] = tile[16 * p : 16 * p + 8]
            xlo[first + p] = tile[16 * p + 8 : 16 * p + 16]


def strip_kernel(d, g, xlo, xhi):
    for k in range(4):
        put(xlo, xhi, 8 * k, [d[8 * k + p] for p in range(8)], False)
    for k in range(2):
        sources = [g[8 * k + 2 * p : 8 * k + 2 * p + 2].reshape(256, 128) for p in range(4)]
        put(xlo, xhi, 34 + 4 * k, sources, True)


def strip_y_kernel(xlo_in, xhi_in, yl, yh, q, q2, xlo, xhi):
    put(xlo, xhi, 32, [yl[0:32].reshape(256, 128), yh[0:32].reshape(256, 128)], False)
    coarse = jnp.concatenate([yl[32:48].reshape(128, 128), yh[32:48].reshape(128, 128)], axis=0)
    put(xlo, xhi, 42, [coarse], True)
    sides = jnp.concatenate([yl[48], yh[48]], axis=1)
    rest = jnp.concatenate([q[...], q2[...]], axis=1)
    xlo[43] = sides
    xlo[44] = rest
    xhi[43] = sides
    xhi[44] = rest


def zstrip_kernel(g, yl, yh, xl, xr, q3, qm, qp, zlo, zhi, own):
    def quarters(ref, i):
        a, b = ref[2 * i], ref[2 * i + 1]
        return [b[:, 0:4], a[:, 0:4], a[:, 128:132], b[:, 128:132]]

    packed = jnp.concatenate(
        sum((quarters(q3, i) for i in range(3)), [])
        + quarters(qm, 1) + quarters(qm, 0) + quarters(qm, 2) + quarters(qp, 1) + quarters(qp, 0),
        axis=1,
    )
    own[...] = packed
    zlo[148] = packed
    zhi[148] = packed
    for out, p0, far in ((zlo, 0, 4), (zhi, 24, 8)):
        for p in range(8):
            for s, src in ((0, xl), (1, xr)):
                for half in range(2):
                    out[p * 4 + s * 2 + half] = src[p0 + p, :, half * 128 : half * 128 + 128]
        out[32:40] = yl[p0 : p0 + 8]
        out[40:48] = yh[p0 : p0 + 8]
        for s, src in ((0, xl), (1, xr)):
            a, b = src[32], src[33]
            out[48 + s] = jnp.concatenate([a[:, p0 * 8 : p0 * 8 + 64], b[:, p0 * 8 : p0 * 8 + 64]], axis=1)
        for i in range(4):
            out[50 + 16 * i : 66 + 16 * i] = g[far + i].reshape(16, 8, 128)
        c0 = 0 if p0 == 0 else 8
        out[114:122] = yl[32 + c0 : 40 + c0]
        out[122:130] = yh[32 + c0 : 40 + c0]
        for b in range(4):
            for s, src in ((0, xl), (1, xr)):
                for half in range(2):
                    out[130 + b * 4 + s * 2 + half] = src[34 + c0 // 2 + b, :, half * 128 : half * 128 + 128]
        for s, src in ((0, xl), (1, xr)):
            a = src[42]
            out[146 + s] = jnp.concatenate(
                [a[:, c0 * 8 : c0 * 8 + 64], a[:, 128 + c0 * 8 : 128 + c0 * 8 + 64]], axis=1
            )


def own_fine_kernel(ft, d, yl, yh, xl, xr, e):
    w = x_weights(ft, False)

    def strip(i):
        return jnp.concatenate([xl[i], xr[i]], axis=0)

    @pl.loop(0, 32, unroll=4)
    def _(z):
        r = x_block(d[z], strip(z), w)
        for t in range(2):
            e[t, z, 8:264, :] = r[:, t * 128 : t * 128 + 128]

    for i, src, row in ((32, yl, 0), (33, yh, 264)):
        r = x_block(src[0:32].reshape(256, 128), strip(i), w).reshape(32, 8, 256)
        for t in range(2):
            e[t, :, row : row + 8, :] = r[:, :, t * 128 : t * 128 + 128]


def own_coarse_kernel(ct, g, yl, yh, xl, xr, ec):
    def strip(i):
        return jnp.concatenate([xl[i], xr[i]], axis=0)

    wc = x_weights(ct, True)

    @pl.loop(0, 8, unroll=4)
    def _(b):
        r = x_block(g[pl.ds(2 * b, 2)].reshape(256, 128), strip(34 + b), wc).reshape(2, 128, 256)
        for t in range(2):
            ec[t, pl.ds(2 * b, 2), 8:136, :] = r[:, :, t * 128 : t * 128 + 128]

    r = x_block(
        jnp.concatenate([yl[32:48].reshape(128, 128), yh[32:48].reshape(128, 128)], axis=0),
        strip(42), wc,
    ).reshape(2, 16, 8, 256)
    for t in range(2):
        ec[t, :, 0:8, :] = r[0, :, :, t * 128 : t * 128 + 128]
        ec[t, :, 136:144, :] = r[1, :, :, t * 128 : t * 128 + 128]


def z_group(planes, taps, t, count):
    w = [jnp.full((8, 128), taps[t, 2, k], f32) for k in range(TAPS)]
    w = [jnp.concatenate([v, v], axis=0) for v in w]
    acc = [None] * count
    for i in range(count + 2 * R):
        v = planes(i)
        for o in range(count):
            k = i - o
            if 0 <= k < TAPS:
                acc[o] = w[k] * v if acc[o] is None else acc[o] + w[k] * v
    return acc


def final_kernel(ft, ct, e, ec, zl, zh, sl, sh, tp, out, eh, ech, gn, fh, fl, fch, fcl):
    w = x_weights(ft, False)

    def strip(ref, i):
        return jnp.concatenate(
            [
                jnp.concatenate([ref[i], ref[i + 1]], axis=1),
                jnp.concatenate([ref[i + 2], ref[i + 3]], axis=1),
            ],
            axis=0,
        )

    for n, (m, s) in enumerate(((zl, sl), (zh, sh))):

        @pl.loop(0, 8, unroll=4)
        def _(p, n=n, m=m, s=s):
            r = x_block(m[p], strip(s, 4 * p), w)
            for t in range(2):
                eh[t, 8 * n + p, 8:264, :] = r[:, t * 128 : t * 128 + 128]

        @pl.loop(0, 4)
        def _(p, n=n, m=m):
            gn[4 * n + p] = pool(m, p)

    def sides(lo, hi):
        return jnp.concatenate([lo, hi], axis=0)

    def pair(i):
        return jnp.concatenate(
            [jnp.concatenate([sl[i], sh[i]], axis=1), jnp.concatenate([sl[i + 1], sh[i + 1]], axis=1)],
            axis=0,
        )

    r = x_block(
        sides(sl[32:48].reshape(128, 128), sh[32:48].reshape(128, 128)), pair(48), w
    ).reshape(2, 2, 8, 8, 256)
    for n in range(2):
        for t in range(2):
            eh[t, 8 * n : 8 * n + 8, 0:8, :] = r[n, 0, :, :, t * 128 : t * 128 + 128]
            eh[t, 8 * n : 8 * n + 8, 264:272, :] = r[n, 1, :, :, t * 128 : t * 128 + 128]

    wc = x_weights(ct, True)
    for n, s in enumerate((sl, sh)):
        for b in range(4):
            near = b >= 2 if n == 0 else b < 2
            if near:
                first = 2 * (b - 2) if n == 0 else 4 + 2 * b
                rows = gn[first : first + 2].reshape(256, 128)
            else:
                first = 50 + 32 * (b if n == 0 else b - 2)
                rows = s[first : first + 32].reshape(256, 128)
            r = x_block(rows, strip(s, 130 + 4 * b), wc).reshape(2, 128, 256)
            for t in range(2):
                ech[t, 8 * n + 2 * b : 8 * n + 2 * b + 2, 8:136, :] = r[:, :, t * 128 : t * 128 + 128]
    r = x_block(
        sides(sl[114:130].reshape(128, 128), sh[114:130].reshape(128, 128)), pair(146), wc
    ).reshape(2, 2, 8, 8, 256)
    for n in range(2):
        for t in range(2):
            ech[t, 8 * n : 8 * n + 8, 0:8, :] = r[n, 0, :, :, t * 128 : t * 128 + 128]
            ech[t, 8 * n : 8 * n + 8, 136:144, :] = r[n, 1, :, :, t * 128 : t * 128 + 128]

    @pl.loop(0, 17)
    def _(y):
        rows = pl.ds(pl.multiple_of(y * 16, 16), 16)
        for t in range(2):
            for zb in range(4):

                def plane(i, t=t, zb=zb):
                    i = i + 8 * zb
                    if i < 8:
                        return eh[t, i, rows, :]
                    if i < 40:
                        return e[t, i - 8, rows, :]
                    return eh[t, i - 32, rows, :]

                for o, v in enumerate(z_group(plane, ft, t, 8)):
                    z = 8 * zb + o
                    q, l, r = z // 4, z // 2 % 2, z % 2
                    hi, lo = split(v)
                    fh[t, 2 * q + r, rows, l * 128 : l * 128 + 128] = hi
                    fl[t, 2 * q + r, rows, l * 128 : l * 128 + 128] = lo

    @pl.loop(0, 9)
    def _(y):
        rows = pl.ds(pl.multiple_of(y * 16, 16), 16)
        for t in range(2):
            for zb in range(2):

                def plane(i, t=t, zb=zb):
                    i = i + 8 * zb
                    if i < 8:
                        return ech[t, i, rows, :]
                    if i < 24:
                        return ec[t, i - 8, rows, :]
                    return ech[t, i - 16, rows, :]

                for o, v in enumerate(z_group(plane, ct, t, 8)):
                    z = 8 * zb + o
                    hi, lo = split(v)
                    fch[t, z // 2, rows, (z % 2) * 128 : (z % 2) * 128 + 128] = hi
                    fcl[t, z // 2, rows, (z % 2) * 128 : (z % 2) * 128 + 128] = lo

    wy, wyc = (
        jnp.concatenate([y_weights(taps, t, coarse) for t in range(2)], axis=1)
        for taps, coarse in ((ft, False), (ct, True))
    )

    def stacked(h, l, index, first, size):
        rows = slice(first, first + size)
        return jnp.concatenate([stack(h[t, index, rows, :], l[t, index, rows, :]) for t in range(2)], axis=0)

    @pl.loop(0, 8)
    def _(q):
        for b in range(4):
            top = jnp.concatenate(
                [jnp.broadcast_to(tp[2 * b + k : 2 * b + k + 1, :], (32, 128)) for k in range(2)], axis=0
            )
            common = mm(wyc, stacked(fch, fcl, q, 32 * b, 48))
            even, odd = common[:, 0:128] + top, common[:, 128:256] + top
            for r in range(2):
                res = mm(wy, stacked(fh, fl, 2 * q + r, 64 * b, 80))
                out[4 * q + r, 64 * b : 64 * b + 64, :] = res[:, 0:128] + even
                out[4 * q + 2 + r, 64 * b : 64 * b + 64, :] = res[:, 128:256] + odd


def sds(*shape):
    return jax.ShapeDtypeStruct(shape, f32)


def call(kernel, outs, n_smem, args, scratch=(), flops=0, nbytes=0, grant=12, alias=None):
    return pl.pallas_call(
        kernel,
        out_shape=outs,
        in_specs=[SM] * n_smem + [VM] * (len(args) - n_smem),
        out_specs=jax.tree.map(lambda _: VM, outs),
        scratch_shapes=scratch,
        compiler_params=pltpu.CompilerParams(vmem_limit_bytes=grant * 1024 * 1024),
        input_output_aliases=alias or {},
        cost_estimate=pl.CostEstimate(flops=flops, bytes_accessed=nbytes, transcendentals=0),
    )(*args)


OFFSETS = {"gx": (0, -1, 1, -4, -3, -2, 2, 3), "gy": (0, -1, 1, 2), "gz": (0, -1, 1, -4, -3, -2, 2, 3)}


def wrapped(d, period):
    d = jnp.abs(d) & (period - 1)
    return jnp.minimum(d, period - d).astype(f32)


def pick(index, values):
    out = jnp.zeros(index.shape, jnp.int32)
    for i, v in enumerate(values):
        out = jnp.where(index == i, v, out)
    return out


def matrix_kernel(k):
    lane = iota((8, 128), 1)
    ys = pick((lane >> 2) & 3, OFFSETS["gy"]) * 8 + iota((8, 128), 0)
    xs = pick(lane >> 4, OFFSETS["gx"]) * 4 + (lane & 3)

    @pl.loop(0, 8)
    def _(y):
        dy = wrapped(y - ys, 32)
        for x in range(4):
            dx = wrapped(x - xs, 32)
            r2 = 1.0 + dy * dy + dx * dx
            for i, off in enumerate(OFFSETS["gz"]):
                dz = float(min(abs(off), 8 - abs(off)))
                k[x, y, i] = 1.0 / (256.0 * jnp.sqrt(r2 + dz * dz))


def top_kernel(k, p3, pm, pp, tp):
    tiles = [p3[0], p3[1], p3[2], pm[1], pm[0], pm[2], pp[1], pp[0]]
    lane = iota((8, 128), 1) >> 5
    out = jnp.zeros((8, 128), f32)
    for x in range(4):
        rows = []
        for y in range(8):
            v = k[x, y, 0] * tiles[0]
            for i in range(1, 8):
                v = v + k[x, y, i] * tiles[i]
            rows.append(jnp.sum(v, axis=0, keepdims=True))
        total = jnp.sum(jnp.concatenate(rows, axis=0), axis=1, keepdims=True)
        out = jnp.where(lane == x, jnp.broadcast_to(total, (8, 128)), out)
    tp[...] = out


def q3_kernel(xlo, xl, xr, q3):
    q3[0:2] = xlo[43:45]
    q3[2:4] = xl[43:45]
    q3[4:6] = xr[43:45]


def p3_kernel(p0, sl, sh, p3):
    p3[0] = p0[...]
    p3[1] = sl[148]
    p3[2] = sh[148]


def body(charges, fine_taps, coarse_taps):
    ft, ct = fine_taps, coarse_taps
    zl = shift(charges[24:32], "gz", 1)
    zh = shift(charges[0:8], "gz", -1)

    g, ylo, yhi, q = call(
        prep_kernel, (sds(16, 128, 128), sds(49, 8, 128), sds(49, 8, 128), sds(8, 128)), 0, (charges,),
        flops=1 << 22, nbytes=6 << 20,
    )
    q2 = shift(q, "gy", 2)
    yl = shift(yhi, "gy", 1)
    yh = shift(ylo, "gy", -1)

    xlo, xhi = call(
        strip_kernel, (sds(NB, 8, 256), sds(NB, 8, 256)), 0, (charges, g),
        flops=1 << 27, nbytes=6 << 20,
    )
    xlo, xhi = call(
        strip_y_kernel, (sds(NB, 8, 256), sds(NB, 8, 256)), 0, (xlo, xhi, yl, yh, q, q2),
        flops=1 << 24, nbytes=1 << 20, alias={0: 0, 1: 1},
    )
    xl = shift(xhi, "gx", 1)
    xr = shift(xlo, "gx", -1)

    k = call(matrix_kernel, sds(4, 8, 8, 8, 128), 0, (), flops=1 << 24, nbytes=1 << 20)
    q3 = call(q3_kernel, sds(6, 8, 256), 0, (xlo, xl, xr))
    qm = shift(q3, "gx", 3)
    qp = shift(q3, "gx", -3)

    zlo, zhi, p0 = call(
        zstrip_kernel, (sds(NT, 8, 128), sds(NT, 8, 128), sds(8, 128)), 0,
        (g, yl, yh, xl, xr, q3, qm, qp), flops=1 << 20, nbytes=4 << 20,
    )
    sl = shift(zhi, "gz", 1)
    sh = shift(zlo, "gz", -1)

    e = call(
        own_fine_kernel, sds(2, 32, 272, 128), 1,
        (ft, charges, yl, yh, xl, xr), flops=5 << 30, nbytes=16 << 20,
    )

    p3 = call(p3_kernel, sds(3, 8, 128), 0, (p0, sl, sh))
    pm = shift(p3, "gz", 3)
    pp = shift(p3, "gz", -3)
    ec = call(
        own_coarse_kernel, sds(2, 16, 144, 128), 1,
        (ct, g, yl, yh, xl, xr), flops=1 << 30, nbytes=4 << 20,
    )
    tp = call(top_kernel, sds(8, 128), 0, (k, p3, pm, pp))

    out = call(
        final_kernel, sds(32, 256, 128), 2, (ft, ct, e, ec, zl, zh, sl, sh, tp),
        scratch=[
            pltpu.VMEM((2, 16, 272, 128), f32),
            pltpu.VMEM((2, 16, 144, 128), f32),
            pltpu.VMEM((8, 128, 128), f32),
            pltpu.VMEM((2, 16, 272, 256), bf16),
            pltpu.VMEM((2, 16, 272, 256), bf16),
            pltpu.VMEM((2, 8, 144, 256), bf16),
            pltpu.VMEM((2, 8, 144, 256), bf16),
        ],
        flops=8 << 30, nbytes=20 << 20, grant=30,
    )
    return out


def solution(mesh):
    return jax.shard_map(
        body,
        mesh=mesh,
        in_specs=(P("gz", "gy", "gx"), P(), P()),
        out_specs=P("gz", "gy", "gx"),
        check_vma=False,
    )
```

```python
import jax
import jax.numpy as jnp
from jax import lax
from jax.experimental import pallas as pl
from jax.experimental.pallas import tpu as pltpu
from jax.sharding import PartitionSpec as P


f32 = jnp.float32
bf16 = jnp.bfloat16
NB = 45
NT = 148
R = 8
TAPS = 17

VM = pl.BlockSpec(memory_space=pltpu.VMEM)
SM = pl.BlockSpec(memory_space=pltpu.SMEM)


def shift(value, axis, step):
    count = lax.axis_size(axis)
    return lax.ppermute(value, axis, [(i, (i + step) % count) for i in range(count)])


def split(a):
    hi = a.astype(bf16)
    lo = (a - hi.astype(f32)).astype(bf16)
    return hi, lo


def mm(a, b):
    return jnp.dot(a, b, preferred_element_type=f32)


def iota(shape, dim):
    return lax.broadcasted_iota(jnp.int32, shape, dim)


def banded(taps, t, axis, delta):
    out = jnp.zeros(delta.shape, f32)
    for k in range(TAPS):
        out = jnp.where(delta == k, taps[t, axis, k], out)
    return out


def x_weights(taps, coarse):
    sh = 1 if coarse else 0
    scale = 0.125 if coarse else 1.0
    edge = 128 >> sh

    def halves(rows, source):
        cols = iota((rows, 128), 1) >> sh
        return jnp.concatenate(
            [banded(taps, t, 0, source - cols + R) * scale for t in range(2)], axis=1
        )

    hi, lo = split(halves(128, iota((128, 128), 0) >> sh))
    h = iota((16, 128), 0)
    hhi, hlo = split(halves(16, jnp.where(h < 8, h - 8, h - 8 + edge)))
    return jnp.concatenate([hi, hi, lo, hhi, hhi, hlo, jnp.zeros((80, 256), bf16)], axis=0)


def y_weights(taps, t, coarse):
    seg = 48 if coarse else 80
    c = iota((64, 256), 1)
    i = iota((64, 256), 0) >> (1 if coarse else 0)
    j = c - jnp.where(c >= seg, seg, 0) - jnp.where(c >= 2 * seg, seg, 0)
    m = jnp.where(c < 3 * seg, banded(taps, t, 1, j - i), 0.0)
    hi = m.astype(bf16).astype(f32)
    return jnp.where(c < 2 * seg, hi, m - hi).astype(bf16)


def stack(hi, lo):
    pad = jnp.zeros((256 - 3 * hi.shape[0], hi.shape[1]), bf16)
    return jnp.concatenate([hi, lo, hi, pad], axis=0)


def x_block(a, xt, w):
    hi, lo = split(a)
    xhi, xlo = split(xt)
    x3 = jnp.concatenate([xhi, xlo, xhi, jnp.zeros((80, 256), bf16)], axis=0)
    return mm(jnp.concatenate([hi, lo, hi, x3.T], axis=1), w)


def pool(ref, z):
    def half(p):
        return ref[p, pl.ds(0, 128, stride=2), :] + ref[p, pl.ds(1, 128, stride=2), :]

    return half(2 * z) + half(2 * z + 1)


def prep_kernel(d, g, ylo, yhi, own):
    def step(z, acc):
        v = pool(d, z)
        g[z] = v
        return acc + v

    total = lax.fori_loop(0, 16, step, jnp.zeros((128, 128), f32))
    rows = jnp.sum(total.reshape(8, 16, 128), axis=1)
    group = jnp.where((iota((128, 128), 0) >> 5) == iota((128, 128), 1), 0.125, 0.0)
    q = jnp.dot(rows, group, precision=lax.Precision.HIGHEST, preferred_element_type=f32)
    ylo[0:32] = d[:, 0:8, :]
    yhi[0:32] = d[:, 248:256, :]
    ylo[32:48] = g[:, 0:8, :]
    yhi[32:48] = g[:, 120:128, :]
    ylo[48] = q
    yhi[48] = q
    own[...] = q


def put(xlo, xhi, first, sources, coarse):
    width = 32 if coarse else 16
    lane = iota((256, 128), 1)
    tile = None
    for p, v in enumerate(sources):
        if coarse:
            v = v + pltpu.roll(v, 127, 1)
        v = pltpu.roll(v, (width * p + width // 2) % 128, 1)
        tile = v if tile is None else jnp.where(lane >= width * p, v, tile)
    tile = tile.T
    for p in range(len(sources)):
        if coarse:
            rows = [tile[32 * p + 2 * i : 32 * p + 2 * i + 1] for i in range(16)]
            xhi[first + p] = jnp.concatenate(rows[0:8], axis=0)
            xlo[first + p] = jnp.concatenate(rows[8:16], axis=0)
        else:
            xhi[first + p] = tile[16 * p : 16 * p + 8]
            xlo[first + p] = tile[16 * p + 8 : 16 * p + 16]


def strip_kernel(d, g, xlo, xhi):
    for k in range(4):
        put(xlo, xhi, 8 * k, [d[8 * k + p] for p in range(8)], False)
    for k in range(2):
        sources = [g[8 * k + 2 * p : 8 * k + 2 * p + 2].reshape(256, 128) for p in range(4)]
        put(xlo, xhi, 34 + 4 * k, sources, True)


def strip_y_kernel(xlo_in, xhi_in, yl, yh, q, q2, xlo, xhi):
    put(xlo, xhi, 32, [yl[0:32].reshape(256, 128), yh[0:32].reshape(256, 128)], False)
    coarse = jnp.concatenate([yl[32:48].reshape(128, 128), yh[32:48].reshape(128, 128)], axis=0)
    put(xlo, xhi, 42, [coarse], True)
    sides = jnp.concatenate([yl[48], yh[48]], axis=1)
    rest = jnp.concatenate([q[...], q2[...]], axis=1)
    xlo[43] = sides
    xlo[44] = rest
    xhi[43] = sides
    xhi[44] = rest


def pack_kernel(q3, qm, qp, own):
    def quarters(ref, i):
        a, b = ref[2 * i], ref[2 * i + 1]
        return [b[:, 0:4], a[:, 0:4], a[:, 128:132], b[:, 128:132]]

    own[...] = jnp.concatenate(
        sum((quarters(q3, i) for i in range(3)), [])
        + quarters(qm, 1) + quarters(qm, 0) + quarters(qm, 2) + quarters(qp, 1) + quarters(qp, 0),
        axis=1,
    )


def zstrip_kernel(g, yl, yh, xl, xr, zlo, zhi):
    for out, p0, far in ((zlo, 0, 4), (zhi, 24, 8)):
        for p in range(8):
            for s, src in ((0, xl), (1, xr)):
                for half in range(2):
                    out[p * 4 + s * 2 + half] = src[p0 + p, :, half * 128 : half * 128 + 128]
        out[32:40] = yl[p0 : p0 + 8]
        out[40:48] = yh[p0 : p0 + 8]
        for s, src in ((0, xl), (1, xr)):
            a, b = src[32], src[33]
            out[48 + s] = jnp.concatenate([a[:, p0 * 8 : p0 * 8 + 64], b[:, p0 * 8 : p0 * 8 + 64]], axis=1)
        for i in range(4):
            out[50 + 16 * i : 66 + 16 * i] = g[far + i].reshape(16, 8, 128)
        c0 = 0 if p0 == 0 else 8
        out[114:122] = yl[32 + c0 : 40 + c0]
        out[122:130] = yh[32 + c0 : 40 + c0]
        for b in range(4):
            for s, src in ((0, xl), (1, xr)):
                for half in range(2):
                    out[130 + b * 4 + s * 2 + half] = src[34 + c0 // 2 + b, :, half * 128 : half * 128 + 128]
        for s, src in ((0, xl), (1, xr)):
            a = src[42]
            out[146 + s] = jnp.concatenate(
                [a[:, c0 * 8 : c0 * 8 + 64], a[:, 128 + c0 * 8 : 128 + c0 * 8 + 64]], axis=1
            )


def own_fine_kernel(ft, d, yl, yh, xl, xr, e):
    w = x_weights(ft, False)

    def strip(i):
        return jnp.concatenate([xl[i], xr[i]], axis=0)

    @pl.loop(0, 32, unroll=4)
    def _(z):
        r = x_block(d[z], strip(z), w)
        for t in range(2):
            e[t, z, 8:264, :] = r[:, t * 128 : t * 128 + 128]

    for i, src, row in ((32, yl, 0), (33, yh, 264)):
        r = x_block(src[0:32].reshape(256, 128), strip(i), w).reshape(32, 8, 256)
        for t in range(2):
            e[t, :, row : row + 8, :] = r[:, :, t * 128 : t * 128 + 128]


def own_coarse(ct, g, yl, yh, xl, xr, ec):
    def strip(i):
        return jnp.concatenate([xl[i], xr[i]], axis=0)

    wc = x_weights(ct, True)

    @pl.loop(0, 8, unroll=4)
    def _(b):
        r = x_block(g[pl.ds(2 * b, 2)].reshape(256, 128), strip(34 + b), wc).reshape(2, 128, 256)
        for t in range(2):
            ec[t, pl.ds(2 * b, 2), 8:136, :] = r[:, :, t * 128 : t * 128 + 128]

    r = x_block(
        jnp.concatenate([yl[32:48].reshape(128, 128), yh[32:48].reshape(128, 128)], axis=0),
        strip(42), wc,
    ).reshape(2, 16, 8, 256)
    for t in range(2):
        ec[t, :, 0:8, :] = r[0, :, :, t * 128 : t * 128 + 128]
        ec[t, :, 136:144, :] = r[1, :, :, t * 128 : t * 128 + 128]


def z_group(planes, taps, t, first, last, acc=None):
    w = [jnp.full((8, 128), taps[t, 2, k], f32) for k in range(TAPS)]
    w = [jnp.concatenate([v, v], axis=0) for v in w]
    acc = [None] * 8 if acc is None else list(acc)
    for i in range(first, last):
        v = planes(i)
        for o in range(8):
            k = i - o
            if 0 <= k < TAPS:
                acc[o] = w[k] * v if acc[o] is None else acc[o] + w[k] * v
    return acc


def put_pair(hi_ref, lo_ref, t, first, rows, values):
    for z, v in enumerate(values):
        q, l, r = z // 4, z // 2 % 2, z % 2
        hi, lo = split(v)
        hi_ref[t, first + 2 * q + r, rows, l * 128 : l * 128 + 128] = hi
        lo_ref[t, first + 2 * q + r, rows, l * 128 : l * 128 + 128] = lo


def inner_kernel(ft, ct, e, g, yl, yh, xl, xr, fih, fil, pa, pc, ec):
    own_coarse(ct, g, yl, yh, xl, xr, ec)

    @pl.loop(0, 17)
    def _(y):
        rows = pl.ds(pl.multiple_of(y * 16, 16), 16)
        for t in range(2):
            for n in range(2):

                def plane(i, t=t, n=n):
                    return e[t, i + 8 * n, rows, :]

                put_pair(fih, fil, t, 4 * n, rows, z_group(plane, ft, t, 0, 24))
            for o, v in enumerate(z_group(lambda i, t=t: e[t, i - 8, rows, :], ft, t, 8, 24)):
                pa[t, 0, o, rows, :] = v
            for o, v in enumerate(z_group(lambda i, t=t: e[t, i + 16, rows, :], ft, t, 0, 16)):
                pa[t, 1, o, rows, :] = v

    @pl.loop(0, 9)
    def _(y):
        rows = pl.ds(pl.multiple_of(y * 16, 16), 16)
        for t in range(2):
            for o, v in enumerate(z_group(lambda i, t=t: ec[t, i - 8, rows, :], ct, t, 8, 24)):
                pc[t, 0, o, rows, :] = v
            for o, v in enumerate(z_group(lambda i, t=t: ec[t, i, rows, :], ct, t, 0, 16)):
                pc[t, 1, o, rows, :] = v


def outer_kernel(ft, ct, pa, pc, zl, zh, sl, sh, fh, fl, fch, fcl, eh, ech, gn):
    w = x_weights(ft, False)

    def strip(ref, i):
        return jnp.concatenate(
            [
                jnp.concatenate([ref[i], ref[i + 1]], axis=1),
                jnp.concatenate([ref[i + 2], ref[i + 3]], axis=1),
            ],
            axis=0,
        )

    for n, (m, s) in enumerate(((zl, sl), (zh, sh))):

        @pl.loop(0, 8, unroll=4)
        def _(p, n=n, m=m, s=s):
            r = x_block(m[p], strip(s, 4 * p), w)
            for t in range(2):
                eh[t, 8 * n + p, 8:264, :] = r[:, t * 128 : t * 128 + 128]

        @pl.loop(0, 4)
        def _(p, n=n, m=m):
            gn[4 * n + p] = pool(m, p)

    def sides(lo, hi):
        return jnp.concatenate([lo, hi], axis=0)

    def pair(i):
        return jnp.concatenate(
            [jnp.concatenate([sl[i], sh[i]], axis=1), jnp.concatenate([sl[i + 1], sh[i + 1]], axis=1)],
            axis=0,
        )

    r = x_block(
        sides(sl[32:48].reshape(128, 128), sh[32:48].reshape(128, 128)), pair(48), w
    ).reshape(2, 2, 8, 8, 256)
    for n in range(2):
        for t in range(2):
            eh[t, 8 * n : 8 * n + 8, 0:8, :] = r[n, 0, :, :, t * 128 : t * 128 + 128]
            eh[t, 8 * n : 8 * n + 8, 264:272, :] = r[n, 1, :, :, t * 128 : t * 128 + 128]

    wc = x_weights(ct, True)
    for n, s in enumerate((sl, sh)):
        for b in range(4):
            near = b >= 2 if n == 0 else b < 2
            if near:
                first = 2 * (b - 2) if n == 0 else 4 + 2 * b
                rows = gn[first : first + 2].reshape(256, 128)
            else:
                first = 50 + 32 * (b if n == 0 else b - 2)
                rows = s[first : first + 32].reshape(256, 128)
            r = x_block(rows, strip(s, 130 + 4 * b), wc).reshape(2, 128, 256)
            for t in range(2):
                ech[t, 8 * n + 2 * b : 8 * n + 2 * b + 2, 8:136, :] = r[:, :, t * 128 : t * 128 + 128]
    r = x_block(
        sides(sl[114:130].reshape(128, 128), sh[114:130].reshape(128, 128)), pair(146), wc
    ).reshape(2, 2, 8, 8, 256)
    for n in range(2):
        for t in range(2):
            ech[t, 8 * n : 8 * n + 8, 0:8, :] = r[n, 0, :, :, t * 128 : t * 128 + 128]
            ech[t, 8 * n : 8 * n + 8, 136:144, :] = r[n, 1, :, :, t * 128 : t * 128 + 128]

    def rest(planes, taps, partial, t, n, rows):
        acc = [partial[t, n, o, rows, :] for o in range(8)]
        first = 16 * n
        return z_group(lambda i: planes[t, 8 * n + i - first, rows, :], taps, t, first, first + 8, acc)

    @pl.loop(0, 17)
    def _(y):
        rows = pl.ds(pl.multiple_of(y * 16, 16), 16)
        for t in range(2):
            for n in range(2):
                put_pair(fh, fl, t, 4 * n, rows, rest(eh, ft, pa, t, n, rows))

    @pl.loop(0, 9)
    def _(y):
        rows = pl.ds(pl.multiple_of(y * 16, 16), 16)
        for t in range(2):
            for n in range(2):
                for o, v in enumerate(rest(ech, ct, pc, t, n, rows)):
                    hi, lo = split(v)
                    cols = slice((o % 2) * 128, (o % 2) * 128 + 128)
                    fch[t, 4 * n + o // 2, rows, cols] = hi
                    fcl[t, 4 * n + o // 2, rows, cols] = lo


def final_kernel(ft, ct, fh, fl, fih, fil, fch, fcl, tp, out):
    wy, wyc = (
        jnp.concatenate([y_weights(taps, t, coarse) for t in range(2)], axis=1)
        for taps, coarse in ((ft, False), (ct, True))
    )

    def stacked(h, l, index, first, size):
        rows = slice(first, first + size)
        return jnp.concatenate([stack(h[t, index, rows, :], l[t, index, rows, :]) for t in range(2)], axis=0)

    def slab(q, h, l, first):
        for b in range(4):
            top = jnp.concatenate(
                [jnp.broadcast_to(tp[2 * b + k : 2 * b + k + 1, :], (32, 128)) for k in range(2)], axis=0
            )
            common = mm(wyc, stacked(fch, fcl, q, 32 * b, 48))
            even, odd = common[:, 0:128] + top, common[:, 128:256] + top
            for r in range(2):
                res = mm(wy, stacked(h, l, first + r, 64 * b, 80))
                out[4 * q + r, 64 * b : 64 * b + 64, :] = res[:, 0:128] + even
                out[4 * q + 2 + r, 64 * b : 64 * b + 64, :] = res[:, 128:256] + odd

    @pl.loop(2, 6)
    def _(q):
        slab(q, fih, fil, 2 * q - 4)

    @pl.loop(0, 2)
    def _(n):
        slab(n, fh, fl, 2 * n)
        slab(6 + n, fh, fl, 4 + 2 * n)


def sds(*shape):
    return jax.ShapeDtypeStruct(shape, f32)


def call(kernel, outs, n_smem, args, scratch=(), flops=0, nbytes=0, grant=12, alias=None):
    return pl.pallas_call(
        kernel,
        out_shape=outs,
        in_specs=[SM] * n_smem + [VM] * (len(args) - n_smem),
        out_specs=jax.tree.map(lambda _: VM, outs),
        scratch_shapes=scratch,
        compiler_params=pltpu.CompilerParams(vmem_limit_bytes=grant * 1024 * 1024),
        input_output_aliases=alias or {},
        cost_estimate=pl.CostEstimate(flops=flops, bytes_accessed=nbytes, transcendentals=0),
    )(*args)


OFFSETS = {"gx": (0, -1, 1, -4, -3, -2, 2, 3), "gy": (0, -1, 1, 2), "gz": (0, -1, 1, -4, -3, -2, 2, 3)}


def wrapped(d, period):
    d = jnp.abs(d) & (period - 1)
    return jnp.minimum(d, period - d).astype(f32)


def pick(index, values):
    out = jnp.zeros(index.shape, jnp.int32)
    for i, v in enumerate(values):
        out = jnp.where(index == i, v, out)
    return out


def matrix_kernel(k):
    lane = iota((8, 128), 1)
    ys = pick((lane >> 2) & 3, OFFSETS["gy"]) * 8 + iota((8, 128), 0)
    xs = pick(lane >> 4, OFFSETS["gx"]) * 4 + (lane & 3)

    @pl.loop(0, 8)
    def _(y):
        dy = wrapped(y - ys, 32)
        for x in range(4):
            dx = wrapped(x - xs, 32)
            r2 = 1.0 + dy * dy + dx * dx
            for i, off in enumerate(OFFSETS["gz"]):
                dz = float(min(abs(off), 8 - abs(off)))
                k[x, y, i] = 1.0 / (256.0 * jnp.sqrt(r2 + dz * dz))


def top_kernel(k, p3, pm, pp, tp):
    tiles = [p3[0], p3[1], p3[2], pm[1], pm[0], pm[2], pp[1], pp[0]]
    lane = iota((8, 128), 1) >> 5
    out = jnp.zeros((8, 128), f32)
    for x in range(4):
        rows = []
        for y in range(8):
            v = k[x, y, 0] * tiles[0]
            for i in range(1, 8):
                v = v + k[x, y, i] * tiles[i]
            rows.append(jnp.sum(v, axis=0, keepdims=True))
        total = jnp.sum(jnp.concatenate(rows, axis=0), axis=1, keepdims=True)
        out = jnp.where(lane == x, jnp.broadcast_to(total, (8, 128)), out)
    tp[...] = out


def q3_kernel(xlo, xl, xr, q3):
    q3[0:2] = xlo[43:45]
    q3[2:4] = xl[43:45]
    q3[4:6] = xr[43:45]


def p3_kernel(p0, sl, sh, p3):
    p3[0] = p0[...]
    p3[1] = sl[...]
    p3[2] = sh[...]


def body(charges, fine_taps, coarse_taps):
    ft, ct = fine_taps, coarse_taps
    zl = shift(charges[24:32], "gz", 1)
    zh = shift(charges[0:8], "gz", -1)

    g, ylo, yhi, q = call(
        prep_kernel, (sds(16, 128, 128), sds(49, 8, 128), sds(49, 8, 128), sds(8, 128)), 0, (charges,),
        flops=1 << 22, nbytes=6 << 20,
    )
    q2 = shift(q, "gy", 2)
    yl = shift(yhi, "gy", 1)
    yh = shift(ylo, "gy", -1)

    xlo, xhi = call(
        strip_kernel, (sds(NB, 8, 256), sds(NB, 8, 256)), 0, (charges, g),
        flops=1 << 27, nbytes=6 << 20,
    )
    xlo, xhi = call(
        strip_y_kernel, (sds(NB, 8, 256), sds(NB, 8, 256)), 0, (xlo, xhi, yl, yh, q, q2),
        flops=1 << 24, nbytes=1 << 20, alias={0: 0, 1: 1},
    )
    xl = shift(xhi, "gx", 1)
    xr = shift(xlo, "gx", -1)

    k = call(matrix_kernel, sds(4, 8, 8, 8, 128), 0, (), flops=1 << 24, nbytes=1 << 20)
    q3 = call(q3_kernel, sds(6, 8, 256), 0, (xlo, xl, xr))
    zlo, zhi = call(
        zstrip_kernel, (sds(NT, 8, 128), sds(NT, 8, 128)), 0, (g, yl, yh, xl, xr),
        flops=1 << 20, nbytes=4 << 20,
    )
    sl = shift(zhi, "gz", 1)
    sh = shift(zlo, "gz", -1)
    qm = shift(q3, "gx", 3)
    qp = shift(q3, "gx", -3)

    e = call(
        own_fine_kernel, sds(2, 32, 272, 128), 1,
        (ft, charges, yl, yh, xl, xr), flops=5 << 30, nbytes=16 << 20,
    )
    p0 = call(pack_kernel, sds(8, 128), 0, (q3, qm, qp))
    pl1 = shift(p0, "gz", 1)
    pr1 = shift(p0, "gz", -1)
    half = jax.ShapeDtypeStruct((2, 8, 272, 256), bf16)
    quarter = jax.ShapeDtypeStruct((2, 8, 144, 256), bf16)
    fih, fil, pa, pc = call(
        inner_kernel, (half, half, sds(2, 2, 8, 272, 128), sds(2, 2, 8, 144, 128)), 2,
        (ft, ct, e, g, yl, yh, xl, xr), scratch=[pltpu.VMEM((2, 16, 144, 128), f32)],
        flops=5 << 30, nbytes=16 << 20,
    )
    p3 = call(p3_kernel, sds(3, 8, 128), 0, (p0, pl1, pr1))
    pm = shift(p3, "gz", 3)
    pp = shift(p3, "gz", -3)
    fh, fl, fch, fcl = call(
        outer_kernel, (half, half, quarter, quarter), 2, (ft, ct, pa, pc, zl, zh, sl, sh),
        scratch=[
            pltpu.VMEM((2, 16, 272, 128), f32),
            pltpu.VMEM((2, 16, 144, 128), f32),
            pltpu.VMEM((8, 128, 128), f32),
        ],
        flops=4 << 30, nbytes=16 << 20, grant=16,
    )
    tp = call(top_kernel, sds(8, 128), 0, (k, p3, pm, pp))
    out = call(
        final_kernel, sds(32, 256, 128), 2, (ft, ct, fh, fl, fih, fil, fch, fcl, tp),
        flops=2 << 30, nbytes=16 << 20,
    )
    return out


def solution(mesh):
    return jax.shard_map(
        body,
        mesh=mesh,
        in_specs=(P("gz", "gy", "gx"), P(), P()),
        out_specs=P("gz", "gy", "gx"),
        check_vma=False,
    )
```

```python
import jax
import jax.numpy as jnp
from jax import lax
from jax.experimental import pallas as pl
from jax.experimental.pallas import tpu as pltpu
from jax.sharding import PartitionSpec as P


f32 = jnp.float32
bf16 = jnp.bfloat16
NB = 45
NT = 148
R = 8
TAPS = 17

VM = pl.BlockSpec(memory_space=pltpu.VMEM)
SM = pl.BlockSpec(memory_space=pltpu.SMEM)


def shift(value, axis, step):
    count = lax.axis_size(axis)
    return lax.ppermute(value, axis, [(i, (i + step) % count) for i in range(count)])


def split(a):
    hi = a.astype(bf16)
    lo = (a - hi.astype(f32)).astype(bf16)
    return hi, lo


def mm(a, b):
    return jnp.dot(a, b, preferred_element_type=f32)


def iota(shape, dim):
    return lax.broadcasted_iota(jnp.int32, shape, dim)


def banded(taps, t, axis, delta):
    out = jnp.zeros(delta.shape, f32)
    for k in range(TAPS):
        out = jnp.where(delta == k, taps[t, axis, k], out)
    return out


def x_weights(taps, coarse):
    sh = 1 if coarse else 0
    scale = 0.125 if coarse else 1.0
    edge = 128 >> sh

    def halves(rows, source):
        cols = iota((rows, 128), 1) >> sh
        return jnp.concatenate(
            [banded(taps, t, 0, source - cols + R) * scale for t in range(2)], axis=1
        )

    hi, lo = split(halves(128, iota((128, 128), 0) >> sh))
    h = iota((16, 128), 0)
    hhi, hlo = split(halves(16, jnp.where(h < 8, h - 8, h - 8 + edge)))
    return jnp.concatenate([hi, hi, lo, hhi, hhi, hlo, jnp.zeros((80, 256), bf16)], axis=0)


def y_weights(taps, t, coarse):
    seg = 48 if coarse else 80
    c = iota((64, 256), 1)
    i = iota((64, 256), 0) >> (1 if coarse else 0)
    j = c - jnp.where(c >= seg, seg, 0) - jnp.where(c >= 2 * seg, seg, 0)
    m = jnp.where(c < 3 * seg, banded(taps, t, 1, j - i), 0.0)
    hi = m.astype(bf16).astype(f32)
    return jnp.where(c < 2 * seg, hi, m - hi).astype(bf16)


def stack(hi, lo):
    pad = jnp.zeros((256 - 3 * hi.shape[0], hi.shape[1]), bf16)
    return jnp.concatenate([hi, lo, hi, pad], axis=0)


def x_block(a, xt, w):
    hi, lo = split(a)
    xhi, xlo = split(xt)
    x3 = jnp.concatenate([xhi, xlo, xhi, jnp.zeros((80, 256), bf16)], axis=0)
    return mm(jnp.concatenate([hi, lo, hi, x3.T], axis=1), w)


def pool(ref, z):
    def half(p):
        return ref[p, pl.ds(0, 128, stride=2), :] + ref[p, pl.ds(1, 128, stride=2), :]

    return half(2 * z) + half(2 * z + 1)


def prep_kernel(d, g, ylo, yhi, own):
    def step(z, acc):
        v = pool(d, z)
        g[z] = v
        return acc + v

    total = lax.fori_loop(0, 16, step, jnp.zeros((128, 128), f32))
    rows = jnp.sum(total.reshape(8, 16, 128), axis=1)
    group = jnp.where((iota((128, 128), 0) >> 5) == iota((128, 128), 1), 0.125, 0.0)
    q = jnp.dot(rows, group, precision=lax.Precision.HIGHEST, preferred_element_type=f32)
    ylo[0:32] = d[:, 0:8, :]
    yhi[0:32] = d[:, 248:256, :]
    ylo[32:48] = g[:, 0:8, :]
    yhi[32:48] = g[:, 120:128, :]
    ylo[48] = q
    yhi[48] = q
    own[...] = q


def put(xlo, xhi, first, sources, coarse):
    width = 32 if coarse else 16
    lane = iota((256, 128), 1)
    tile = None
    for p, v in enumerate(sources):
        if coarse:
            v = v + pltpu.roll(v, 127, 1)
        v = pltpu.roll(v, (width * p + width // 2) % 128, 1)
        tile = v if tile is None else jnp.where(lane >= width * p, v, tile)
    tile = tile.T
    for p in range(len(sources)):
        if coarse:
            rows = [tile[32 * p + 2 * i : 32 * p + 2 * i + 1] for i in range(16)]
            xhi[first + p] = jnp.concatenate(rows[0:8], axis=0)
            xlo[first + p] = jnp.concatenate(rows[8:16], axis=0)
        else:
            xhi[first + p] = tile[16 * p : 16 * p + 8]
            xlo[first + p] = tile[16 * p + 8 : 16 * p + 16]


def strip_kernel(d, g, xlo, xhi):
    for k in range(4):
        put(xlo, xhi, 8 * k, [d[8 * k + p] for p in range(8)], False)
    for k in range(2):
        sources = [g[8 * k + 2 * p : 8 * k + 2 * p + 2].reshape(256, 128) for p in range(4)]
        put(xlo, xhi, 34 + 4 * k, sources, True)


def strip_y_kernel(xlo_in, xhi_in, yl, yh, q, q2, xlo, xhi):
    put(xlo, xhi, 32, [yl[0:32].reshape(256, 128), yh[0:32].reshape(256, 128)], False)
    coarse = jnp.concatenate([yl[32:48].reshape(128, 128), yh[32:48].reshape(128, 128)], axis=0)
    put(xlo, xhi, 42, [coarse], True)
    sides = jnp.concatenate([yl[48], yh[48]], axis=1)
    rest = jnp.concatenate([q[...], q2[...]], axis=1)
    xlo[43] = sides
    xlo[44] = rest
    xhi[43] = sides
    xhi[44] = rest


def pack_kernel(q3, qm, qp, own):
    def quarters(ref, i):
        a, b = ref[2 * i], ref[2 * i + 1]
        return [b[:, 0:4], a[:, 0:4], a[:, 128:132], b[:, 128:132]]

    own[...] = jnp.concatenate(
        sum((quarters(q3, i) for i in range(3)), [])
        + quarters(qm, 1) + quarters(qm, 0) + quarters(qm, 2) + quarters(qp, 1) + quarters(qp, 0),
        axis=1,
    )


def zstrip_kernel(g, yl, yh, xl, xr, zlo, zhi):
    for out, p0, far in ((zlo, 0, 4), (zhi, 24, 8)):
        for p in range(8):
            for s, src in ((0, xl), (1, xr)):
                for half in range(2):
                    out[p * 4 + s * 2 + half] = src[p0 + p, :, half * 128 : half * 128 + 128]
        out[32:40] = yl[p0 : p0 + 8]
        out[40:48] = yh[p0 : p0 + 8]
        for s, src in ((0, xl), (1, xr)):
            a, b = src[32], src[33]
            out[48 + s] = jnp.concatenate([a[:, p0 * 8 : p0 * 8 + 64], b[:, p0 * 8 : p0 * 8 + 64]], axis=1)
        for i in range(4):
            out[50 + 16 * i : 66 + 16 * i] = g[far + i].reshape(16, 8, 128)
        c0 = 0 if p0 == 0 else 8
        out[114:122] = yl[32 + c0 : 40 + c0]
        out[122:130] = yh[32 + c0 : 40 + c0]
        for b in range(4):
            for s, src in ((0, xl), (1, xr)):
                for half in range(2):
                    out[130 + b * 4 + s * 2 + half] = src[34 + c0 // 2 + b, :, half * 128 : half * 128 + 128]
        for s, src in ((0, xl), (1, xr)):
            a = src[42]
            out[146 + s] = jnp.concatenate(
                [a[:, c0 * 8 : c0 * 8 + 64], a[:, 128 + c0 * 8 : 128 + c0 * 8 + 64]], axis=1
            )


def own_fine_kernel(wref, d, yl, yh, xl, xr, e):
    w = wref[...]

    def strip(i):
        return jnp.concatenate([xl[i], xr[i]], axis=0)

    @pl.loop(0, 32, unroll=4)
    def _(z):
        r = x_block(d[z], strip(z), w)
        for t in range(2):
            e[t, z, 8:264, :] = r[:, t * 128 : t * 128 + 128]

    for i, src, row in ((32, yl, 0), (33, yh, 264)):
        r = x_block(src[0:32].reshape(256, 128), strip(i), w).reshape(32, 8, 256)
        for t in range(2):
            e[t, :, row : row + 8, :] = r[:, :, t * 128 : t * 128 + 128]


def own_coarse(wcref, g, yl, yh, xl, xr, ec):
    def strip(i):
        return jnp.concatenate([xl[i], xr[i]], axis=0)

    wc = wcref[...]

    @pl.loop(0, 8, unroll=4)
    def _(b):
        r = x_block(g[pl.ds(2 * b, 2)].reshape(256, 128), strip(34 + b), wc).reshape(2, 128, 256)
        for t in range(2):
            ec[t, pl.ds(2 * b, 2), 8:136, :] = r[:, :, t * 128 : t * 128 + 128]

    r = x_block(
        jnp.concatenate([yl[32:48].reshape(128, 128), yh[32:48].reshape(128, 128)], axis=0),
        strip(42), wc,
    ).reshape(2, 16, 8, 256)
    for t in range(2):
        ec[t, :, 0:8, :] = r[0, :, :, t * 128 : t * 128 + 128]
        ec[t, :, 136:144, :] = r[1, :, :, t * 128 : t * 128 + 128]


def z_group(planes, taps, t, first, last, acc=None):
    w = [jnp.full((8, 128), taps[t, 2, k], f32) for k in range(TAPS)]
    w = [jnp.concatenate([v, v], axis=0) for v in w]
    acc = [None] * 8 if acc is None else list(acc)
    for i in range(first, last):
        v = planes(i)
        for o in range(8):
            k = i - o
            if 0 <= k < TAPS:
                acc[o] = w[k] * v if acc[o] is None else acc[o] + w[k] * v
    return acc


def put_pair(hi_ref, lo_ref, t, first, rows, values):
    for z, v in enumerate(values):
        q, l, r = z // 4, z // 2 % 2, z % 2
        hi, lo = split(v)
        hi_ref[t, first + 2 * q + r, rows, l * 128 : l * 128 + 128] = hi
        lo_ref[t, first + 2 * q + r, rows, l * 128 : l * 128 + 128] = lo


def inner_kernel(ft, ct, wcref, e, g, yl, yh, xl, xr, fih, fil, pa, pc, ec):
    own_coarse(wcref, g, yl, yh, xl, xr, ec)

    @pl.loop(0, 17)
    def _(y):
        rows = pl.ds(pl.multiple_of(y * 16, 16), 16)
        for t in range(2):
            for n in range(2):

                def plane(i, t=t, n=n):
                    return e[t, i + 8 * n, rows, :]

                put_pair(fih, fil, t, 4 * n, rows, z_group(plane, ft, t, 0, 24))
            for o, v in enumerate(z_group(lambda i, t=t: e[t, i - 8, rows, :], ft, t, 8, 24)):
                pa[t, 0, o, rows, :] = v
            for o, v in enumerate(z_group(lambda i, t=t: e[t, i + 16, rows, :], ft, t, 0, 16)):
                pa[t, 1, o, rows, :] = v

    @pl.loop(0, 9)
    def _(y):
        rows = pl.ds(pl.multiple_of(y * 16, 16), 16)
        for t in range(2):
            for o, v in enumerate(z_group(lambda i, t=t: ec[t, i - 8, rows, :], ct, t, 8, 24)):
                pc[t, 0, o, rows, :] = v
            for o, v in enumerate(z_group(lambda i, t=t: ec[t, i, rows, :], ct, t, 0, 16)):
                pc[t, 1, o, rows, :] = v


def outer_kernel(ft, ct, wref, wcref, pa, pc, zl, zh, sl, sh, fh, fl, fch, fcl, eh, ech, gn):
    w = wref[...]

    def strip(ref, i):
        return jnp.concatenate(
            [
                jnp.concatenate([ref[i], ref[i + 1]], axis=1),
                jnp.concatenate([ref[i + 2], ref[i + 3]], axis=1),
            ],
            axis=0,
        )

    for n, (m, s) in enumerate(((zl, sl), (zh, sh))):

        @pl.loop(0, 8, unroll=4)
        def _(p, n=n, m=m, s=s):
            r = x_block(m[p], strip(s, 4 * p), w)
            for t in range(2):
                eh[t, 8 * n + p, 8:264, :] = r[:, t * 128 : t * 128 + 128]

        @pl.loop(0, 4)
        def _(p, n=n, m=m):
            gn[4 * n + p] = pool(m, p)

    def sides(lo, hi):
        return jnp.concatenate([lo, hi], axis=0)

    def pair(i):
        return jnp.concatenate(
            [jnp.concatenate([sl[i], sh[i]], axis=1), jnp.concatenate([sl[i + 1], sh[i + 1]], axis=1)],
            axis=0,
        )

    r = x_block(
        sides(sl[32:48].reshape(128, 128), sh[32:48].reshape(128, 128)), pair(48), w
    ).reshape(2, 2, 8, 8, 256)
    for n in range(2):
        for t in range(2):
            eh[t, 8 * n : 8 * n + 8, 0:8, :] = r[n, 0, :, :, t * 128 : t * 128 + 128]
            eh[t, 8 * n : 8 * n + 8, 264:272, :] = r[n, 1, :, :, t * 128 : t * 128 + 128]

    wc = wcref[...]
    for n, s in enumerate((sl, sh)):
        for b in range(4):
            near = b >= 2 if n == 0 else b < 2
            if near:
                first = 2 * (b - 2) if n == 0 else 4 + 2 * b
                rows = gn[first : first + 2].reshape(256, 128)
            else:
                first = 50 + 32 * (b if n == 0 else b - 2)
                rows = s[first : first + 32].reshape(256, 128)
            r = x_block(rows, strip(s, 130 + 4 * b), wc).reshape(2, 128, 256)
            for t in range(2):
                ech[t, 8 * n + 2 * b : 8 * n + 2 * b + 2, 8:136, :] = r[:, :, t * 128 : t * 128 + 128]
    r = x_block(
        sides(sl[114:130].reshape(128, 128), sh[114:130].reshape(128, 128)), pair(146), wc
    ).reshape(2, 2, 8, 8, 256)
    for n in range(2):
        for t in range(2):
            ech[t, 8 * n : 8 * n + 8, 0:8, :] = r[n, 0, :, :, t * 128 : t * 128 + 128]
            ech[t, 8 * n : 8 * n + 8, 136:144, :] = r[n, 1, :, :, t * 128 : t * 128 + 128]

    def rest(planes, taps, partial, t, n, rows):
        acc = [partial[t, n, o, rows, :] for o in range(8)]
        first = 16 * n
        return z_group(lambda i: planes[t, 8 * n + i - first, rows, :], taps, t, first, first + 8, acc)

    @pl.loop(0, 17)
    def _(y):
        rows = pl.ds(pl.multiple_of(y * 16, 16), 16)
        for t in range(2):
            for n in range(2):
                put_pair(fh, fl, t, 4 * n, rows, rest(eh, ft, pa, t, n, rows))

    @pl.loop(0, 9)
    def _(y):
        rows = pl.ds(pl.multiple_of(y * 16, 16), 16)
        for t in range(2):
            for n in range(2):
                for o, v in enumerate(rest(ech, ct, pc, t, n, rows)):
                    hi, lo = split(v)
                    cols = slice((o % 2) * 128, (o % 2) * 128 + 128)
                    fch[t, 4 * n + o // 2, rows, cols] = hi
                    fcl[t, 4 * n + o // 2, rows, cols] = lo


def weights_kernel(ft, ct, w, wc, wy, wyc):
    w[...] = x_weights(ft, False)
    wc[...] = x_weights(ct, True)
    for t in range(2):
        wy[:, t * 256 : t * 256 + 256] = y_weights(ft, t, False)
        wyc[:, t * 256 : t * 256 + 256] = y_weights(ct, t, True)


def final_kernel(wyref, wycref, fh, fl, fih, fil, fch, fcl, tp, out_hbm, out, sems):
    wy, wyc = wyref[...], wycref[...]

    def stacked(h, l, index, first, size):
        rows = slice(first, first + size)
        return jnp.concatenate([stack(h[t, index, rows, :], l[t, index, rows, :]) for t in range(2)], axis=0)

    def slab(q, h, l, first):
        for b in range(4):
            top = jnp.concatenate(
                [jnp.broadcast_to(tp[2 * b + k : 2 * b + k + 1, :], (32, 128)) for k in range(2)], axis=0
            )
            common = mm(wyc, stacked(fch, fcl, q, 32 * b, 48))
            even, odd = common[:, 0:128] + top, common[:, 128:256] + top
            for r in range(2):
                res = mm(wy, stacked(h, l, first + r, 64 * b, 80))
                out[4 * q + r, 64 * b : 64 * b + 64, :] = res[:, 0:128] + even
                out[4 * q + 2 + r, 64 * b : 64 * b + 64, :] = res[:, 128:256] + odd

    def leave(q):
        planes = pl.ds(4 * q, 4)
        return pltpu.make_async_copy(out.at[planes], out_hbm.at[planes], sems.at[q])

    @pl.loop(2, 6)
    def _(q):
        slab(q, fih, fil, 2 * q - 4)
        leave(q).start()

    @pl.loop(0, 2)
    def _(n):
        slab(n, fh, fl, 2 * n)
        leave(n).start()
        slab(6 + n, fh, fl, 4 + 2 * n)
        leave(6 + n).start()

    for q in range(8):
        leave(q).wait()


def sds(*shape):
    return jax.ShapeDtypeStruct(shape, f32)


def call(kernel, outs, n_smem, args, scratch=(), flops=0, nbytes=0, grant=12, alias=None, space=VM):
    return pl.pallas_call(
        kernel,
        out_shape=outs,
        in_specs=[SM] * n_smem + [VM] * (len(args) - n_smem),
        out_specs=jax.tree.map(lambda _: space, outs),
        scratch_shapes=scratch,
        compiler_params=pltpu.CompilerParams(vmem_limit_bytes=grant * 1024 * 1024),
        input_output_aliases=alias or {},
        cost_estimate=pl.CostEstimate(flops=flops, bytes_accessed=nbytes, transcendentals=0),
    )(*args)


OFFSETS = {"gx": (0, -1, 1, -4, -3, -2, 2, 3), "gy": (0, -1, 1, 2), "gz": (0, -1, 1, -4, -3, -2, 2, 3)}


def wrapped(d, period):
    d = jnp.abs(d) & (period - 1)
    return jnp.minimum(d, period - d).astype(f32)


def pick(index, values):
    out = jnp.zeros(index.shape, jnp.int32)
    for i, v in enumerate(values):
        out = jnp.where(index == i, v, out)
    return out


def matrix_kernel(k):
    lane = iota((8, 128), 1)
    ys = pick((lane >> 2) & 3, OFFSETS["gy"]) * 8 + iota((8, 128), 0)
    xs = pick(lane >> 4, OFFSETS["gx"]) * 4 + (lane & 3)

    @pl.loop(0, 8)
    def _(y):
        dy = wrapped(y - ys, 32)
        for x in range(4):
            dx = wrapped(x - xs, 32)
            r2 = 1.0 + dy * dy + dx * dx
            for i, off in enumerate(OFFSETS["gz"]):
                dz = float(min(abs(off), 8 - abs(off)))
                k[x, y, i] = 1.0 / (256.0 * jnp.sqrt(r2 + dz * dz))


def top_kernel(k, p3, pm, pp, tp):
    tiles = [p3[0], p3[1], p3[2], pm[1], pm[0], pm[2], pp[1], pp[0]]
    lane = iota((8, 128), 1) >> 5
    out = jnp.zeros((8, 128), f32)
    for x in range(4):
        rows = []
        for y in range(8):
            v = k[x, y, 0] * tiles[0]
            for i in range(1, 8):
                v = v + k[x, y, i] * tiles[i]
            rows.append(jnp.sum(v, axis=0, keepdims=True))
        total = jnp.sum(jnp.concatenate(rows, axis=0), axis=1, keepdims=True)
        out = jnp.where(lane == x, jnp.broadcast_to(total, (8, 128)), out)
    tp[...] = out


def q3_kernel(xlo, xl, xr, q3):
    q3[0:2] = xlo[43:45]
    q3[2:4] = xl[43:45]
    q3[4:6] = xr[43:45]


def p3_kernel(p0, sl, sh, p3):
    p3[0] = p0[...]
    p3[1] = sl[...]
    p3[2] = sh[...]


def body(charges, fine_taps, coarse_taps):
    ft, ct = fine_taps, coarse_taps
    zl = shift(charges[24:32], "gz", 1)
    zh = shift(charges[0:8], "gz", -1)

    g, ylo, yhi, q = call(
        prep_kernel, (sds(16, 128, 128), sds(49, 8, 128), sds(49, 8, 128), sds(8, 128)), 0, (charges,),
        flops=1 << 22, nbytes=6 << 20,
    )
    q2 = shift(q, "gy", 2)
    yl = shift(yhi, "gy", 1)
    yh = shift(ylo, "gy", -1)

    xlo, xhi = call(
        strip_kernel, (sds(NB, 8, 256), sds(NB, 8, 256)), 0, (charges, g),
        flops=1 << 27, nbytes=6 << 20,
    )
    xlo, xhi = call(
        strip_y_kernel, (sds(NB, 8, 256), sds(NB, 8, 256)), 0, (xlo, xhi, yl, yh, q, q2),
        flops=1 << 24, nbytes=1 << 20, alias={0: 0, 1: 1},
    )
    xl = shift(xhi, "gx", 1)
    xr = shift(xlo, "gx", -1)

    k = call(matrix_kernel, sds(4, 8, 8, 8, 128), 0, (), flops=1 << 24, nbytes=1 << 20)
    wide, tall = (jax.ShapeDtypeStruct(v, bf16) for v in ((64, 512), (512, 256)))
    w, wc, wy, wyc = call(weights_kernel, (tall, tall, wide, wide), 2, (ft, ct), flops=1 << 24, nbytes=1 << 20)
    q3 = call(q3_kernel, sds(6, 8, 256), 0, (xlo, xl, xr))
    zlo, zhi = call(
        zstrip_kernel, (sds(NT, 8, 128), sds(NT, 8, 128)), 0, (g, yl, yh, xl, xr),
        flops=1 << 20, nbytes=4 << 20,
    )
    sl = shift(zhi, "gz", 1)
    sh = shift(zlo, "gz", -1)
    qm = shift(q3, "gx", 3)
    qp = shift(q3, "gx", -3)

    e = call(
        own_fine_kernel, sds(2, 32, 272, 128), 0,
        (w, charges, yl, yh, xl, xr), flops=5 << 30, nbytes=16 << 20,
    )
    p0 = call(pack_kernel, sds(8, 128), 0, (q3, qm, qp))
    pl1 = shift(p0, "gz", 1)
    pr1 = shift(p0, "gz", -1)
    half = jax.ShapeDtypeStruct((2, 8, 272, 256), bf16)
    quarter = jax.ShapeDtypeStruct((2, 8, 144, 256), bf16)
    fih, fil, pa, pc = call(
        inner_kernel, (half, half, sds(2, 2, 8, 272, 128), sds(2, 2, 8, 144, 128)), 2,
        (ft, ct, wc, e, g, yl, yh, xl, xr), scratch=[pltpu.VMEM((2, 16, 144, 128), f32)],
        flops=5 << 30, nbytes=16 << 20,
    )
    p3 = call(p3_kernel, sds(3, 8, 128), 0, (p0, pl1, pr1))
    pm = shift(p3, "gz", 3)
    pp = shift(p3, "gz", -3)
    fh, fl, fch, fcl = call(
        outer_kernel, (half, half, quarter, quarter), 2, (ft, ct, w, wc, pa, pc, zl, zh, sl, sh),
        scratch=[
            pltpu.VMEM((2, 16, 272, 128), f32),
            pltpu.VMEM((2, 16, 144, 128), f32),
            pltpu.VMEM((8, 128, 128), f32),
        ],
        flops=4 << 30, nbytes=16 << 20, grant=16,
    )
    tp = call(top_kernel, sds(8, 128), 0, (k, p3, pm, pp))
    out = call(
        final_kernel, sds(32, 256, 128), 0, (wy, wyc, fh, fl, fih, fil, fch, fcl, tp),
        scratch=[pltpu.VMEM((32, 256, 128), f32), pltpu.SemaphoreType.DMA((8,))],
        flops=2 << 30, nbytes=16 << 20, grant=16, space=pl.BlockSpec(memory_space=pl.ANY),
    )
    return out


def solution(mesh):
    return jax.shard_map(
        body,
        mesh=mesh,
        in_specs=(P("gz", "gy", "gx"), P(), P()),
        out_specs=P("gz", "gy", "gx"),
        check_vma=False,
    )
```

```python
import jax
import jax.numpy as jnp
from jax import lax
from jax.experimental import pallas as pl
from jax.experimental.pallas import tpu as pltpu
from jax.sharding import PartitionSpec as P


f32 = jnp.float32
bf16 = jnp.bfloat16
NB = 40
NT = 148
R = 8
TAPS = 17

VM = pl.BlockSpec(memory_space=pltpu.VMEM)
SM = pl.BlockSpec(memory_space=pltpu.SMEM)


def shift(value, axis, step):
    count = lax.axis_size(axis)
    return lax.ppermute(value, axis, [(i, (i + step) % count) for i in range(count)])


def split(a):
    hi = a.astype(bf16)
    lo = (a - hi.astype(f32)).astype(bf16)
    return hi, lo


def mm(a, b):
    return jnp.dot(a, b, preferred_element_type=f32)


def iota(shape, dim):
    return lax.broadcasted_iota(jnp.int32, shape, dim)


def banded(taps, t, axis, delta):
    out = jnp.zeros(delta.shape, f32)
    for k in range(TAPS):
        out = jnp.where(delta == k, taps[t, axis, k], out)
    return out


def x_weights(taps, coarse):
    sh = 1 if coarse else 0
    scale = 0.125 if coarse else 1.0
    edge = 128 >> sh

    def halves(rows, source):
        cols = iota((rows, 128), 1) >> sh
        return jnp.concatenate(
            [banded(taps, t, 0, source - cols + R) * scale for t in range(2)], axis=1
        )

    hi, lo = split(halves(128, iota((128, 128), 0) >> sh))
    h = iota((16, 128), 0)
    hhi, hlo = split(halves(16, jnp.where(h < 8, h - 8, h - 8 + edge)))
    return jnp.concatenate([hi, hi, lo, hhi, hhi, hlo, jnp.zeros((80, 256), bf16)], axis=0)


def y_weights(taps, t, coarse):
    seg = 48 if coarse else 80
    c = iota((64, 256), 1)
    i = iota((64, 256), 0) >> (1 if coarse else 0)
    j = c - jnp.where(c >= seg, seg, 0) - jnp.where(c >= 2 * seg, seg, 0)
    m = jnp.where(c < 3 * seg, banded(taps, t, 1, j - i), 0.0)
    hi = m.astype(bf16).astype(f32)
    return jnp.where(c < 2 * seg, hi, m - hi).astype(bf16)


def stack(hi, lo):
    pad = jnp.zeros((256 - 3 * hi.shape[0], hi.shape[1]), bf16)
    return jnp.concatenate([hi, lo, hi, pad], axis=0)


def x_block(a, xt, w):
    hi, lo = split(a)
    xhi, xlo = split(xt)
    x3 = jnp.concatenate([xhi, xlo, xhi, jnp.zeros((80, 256), bf16)], axis=0)
    return mm(jnp.concatenate([hi, lo, hi, x3.T], axis=1), w)


def pool(ref, z):
    def half(p):
        return ref[p, pl.ds(0, 128, stride=2), :] + ref[p, pl.ds(1, 128, stride=2), :]

    return half(2 * z) + half(2 * z + 1)


def prep_kernel(d, g, ylo, yhi, own):
    def step(z, acc):
        v = pool(d, z)
        g[z] = v
        return acc + v

    total = lax.fori_loop(0, 16, step, jnp.zeros((128, 128), f32))
    rows = jnp.sum(total.reshape(8, 16, 128), axis=1)
    group = jnp.where((iota((128, 128), 0) >> 5) == iota((128, 128), 1), 0.125, 0.0)
    q = jnp.dot(rows, group, precision=lax.Precision.HIGHEST, preferred_element_type=f32)
    ylo[0:32] = d[:, 0:8, :]
    yhi[0:32] = d[:, 248:256, :]
    ylo[32:48] = g[:, 0:8, :]
    yhi[32:48] = g[:, 120:128, :]
    ylo[48] = q
    yhi[48] = q
    own[...] = q


def put(xlo, xhi, first, sources, coarse):
    width = 32 if coarse else 16
    lane = iota((256, 128), 1)
    tile = None
    for p, v in enumerate(sources):
        if coarse:
            v = v + pltpu.roll(v, 127, 1)
        v = pltpu.roll(v, (width * p + width // 2) % 128, 1)
        tile = v if tile is None else jnp.where(lane >= width * p, v, tile)
    tile = tile.T
    for p in range(len(sources)):
        if coarse:
            rows = [tile[32 * p + 2 * i : 32 * p + 2 * i + 1] for i in range(16)]
            xhi[first + p] = jnp.concatenate(rows[0:8], axis=0)
            xlo[first + p] = jnp.concatenate(rows[8:16], axis=0)
        else:
            xhi[first + p] = tile[16 * p : 16 * p + 8]
            xlo[first + p] = tile[16 * p + 8 : 16 * p + 16]


def strip_kernel(d, g, xlo, xhi):
    for k in range(4):
        put(xlo, xhi, 8 * k, [d[8 * k + p] for p in range(8)], False)
    for k in range(2):
        sources = [g[8 * k + 2 * p : 8 * k + 2 * p + 2].reshape(256, 128) for p in range(4)]
        put(xlo, xhi, 32 + 4 * k, sources, True)


def strip_y_kernel(yl, yh, q, q2, xlo, xhi):
    put(xlo, xhi, 0, [yl[0:32].reshape(256, 128), yh[0:32].reshape(256, 128)], False)
    coarse = jnp.concatenate([yl[32:48].reshape(128, 128), yh[32:48].reshape(128, 128)], axis=0)
    put(xlo, xhi, 2, [coarse], True)
    sides = jnp.concatenate([yl[48], yh[48]], axis=1)
    rest = jnp.concatenate([q[...], q2[...]], axis=1)
    xlo[3] = sides
    xlo[4] = rest
    xhi[3] = sides
    xhi[4] = rest


def pack_kernel(q3, qm, qp, own):
    def quarters(ref, i):
        a, b = ref[2 * i], ref[2 * i + 1]
        return [b[:, 0:4], a[:, 0:4], a[:, 128:132], b[:, 128:132]]

    own[...] = jnp.concatenate(
        sum((quarters(q3, i) for i in range(3)), [])
        + quarters(qm, 1) + quarters(qm, 0) + quarters(qm, 2) + quarters(qp, 1) + quarters(qp, 0),
        axis=1,
    )


def zstrip_kernel(g, yl, yh, xl, xr, cl, cr, zlo, zhi):
    for out, p0, far in ((zlo, 0, 4), (zhi, 24, 8)):
        for p in range(8):
            for s, src in ((0, xl), (1, xr)):
                for half in range(2):
                    out[p * 4 + s * 2 + half] = src[p0 + p, :, half * 128 : half * 128 + 128]
        out[32:40] = yl[p0 : p0 + 8]
        out[40:48] = yh[p0 : p0 + 8]
        for s, src in ((0, cl), (1, cr)):
            a, b = src[0], src[1]
            out[48 + s] = jnp.concatenate([a[:, p0 * 8 : p0 * 8 + 64], b[:, p0 * 8 : p0 * 8 + 64]], axis=1)
        for i in range(4):
            out[50 + 16 * i : 66 + 16 * i] = g[far + i].reshape(16, 8, 128)
        c0 = 0 if p0 == 0 else 8
        out[114:122] = yl[32 + c0 : 40 + c0]
        out[122:130] = yh[32 + c0 : 40 + c0]
        for b in range(4):
            for s, src in ((0, xl), (1, xr)):
                for half in range(2):
                    out[130 + b * 4 + s * 2 + half] = src[32 + c0 // 2 + b, :, half * 128 : half * 128 + 128]
        for s, src in ((0, cl), (1, cr)):
            a = src[2]
            out[146 + s] = jnp.concatenate(
                [a[:, c0 * 8 : c0 * 8 + 64], a[:, 128 + c0 * 8 : 128 + c0 * 8 + 64]], axis=1
            )


def own_fine_kernel(wref, d, xl, xr, e):
    w = wref[...]

    @pl.loop(0, 32, unroll=4)
    def _(z):
        r = x_block(d[z], jnp.concatenate([xl[z], xr[z]], axis=0), w)
        for t in range(2):
            e[t, z, 8:264, :] = r[:, t * 128 : t * 128 + 128]


def own_y_kernel(e_in, wref, yl, yh, cl, cr, e):
    w = wref[...]
    for i, src, row in ((0, yl, 0), (1, yh, 264)):
        strip = jnp.concatenate([cl[i], cr[i]], axis=0)
        r = x_block(src[0:32].reshape(256, 128), strip, w).reshape(32, 8, 256)
        for t in range(2):
            e[t, :, row : row + 8, :] = r[:, :, t * 128 : t * 128 + 128]


def own_coarse(wcref, g, yl, yh, xl, xr, cl, cr, ec):
    def strip(i):
        return jnp.concatenate([xl[i], xr[i]], axis=0)

    wc = wcref[...]

    @pl.loop(0, 8, unroll=4)
    def _(b):
        r = x_block(g[pl.ds(2 * b, 2)].reshape(256, 128), strip(32 + b), wc).reshape(2, 128, 256)
        for t in range(2):
            ec[t, pl.ds(2 * b, 2), 8:136, :] = r[:, :, t * 128 : t * 128 + 128]

    r = x_block(
        jnp.concatenate([yl[32:48].reshape(128, 128), yh[32:48].reshape(128, 128)], axis=0),
        jnp.concatenate([cl[2], cr[2]], axis=0), wc,
    ).reshape(2, 16, 8, 256)
    for t in range(2):
        ec[t, :, 0:8, :] = r[0, :, :, t * 128 : t * 128 + 128]
        ec[t, :, 136:144, :] = r[1, :, :, t * 128 : t * 128 + 128]


def z_group(planes, taps, t, first, last, acc=None):
    w = [jnp.full((8, 128), taps[t, 2, k], f32) for k in range(TAPS)]
    w = [jnp.concatenate([v, v], axis=0) for v in w]
    acc = [None] * 8 if acc is None else list(acc)
    for i in range(first, last):
        v = planes(i)
        for o in range(8):
            k = i - o
            if 0 <= k < TAPS:
                acc[o] = w[k] * v if acc[o] is None else acc[o] + w[k] * v
    return acc


def put_pair(hi_ref, lo_ref, t, first, rows, values):
    for z, v in enumerate(values):
        q, l, r = z // 4, z // 2 % 2, z % 2
        hi, lo = split(v)
        hi_ref[t, first + 2 * q + r, rows, l * 128 : l * 128 + 128] = hi
        lo_ref[t, first + 2 * q + r, rows, l * 128 : l * 128 + 128] = lo


def inner_kernel(ft, e, fih, fil):
    @pl.loop(0, 17)
    def _(y):
        rows = pl.ds(pl.multiple_of(y * 16, 16), 16)
        for t in range(2):
            for n in range(2):

                def plane(i, t=t, n=n):
                    return e[t, i + 8 * n, rows, :]

                put_pair(fih, fil, t, 4 * n, rows, z_group(plane, ft, t, 0, 24))


def partial_kernel(ft, ct, wcref, e, g, yl, yh, xl, xr, cl, cr, pa, pc, ec):
    own_coarse(wcref, g, yl, yh, xl, xr, cl, cr, ec)

    @pl.loop(0, 17)
    def _(y):
        rows = pl.ds(pl.multiple_of(y * 16, 16), 16)
        for t in range(2):
            for o, v in enumerate(z_group(lambda i, t=t: e[t, i - 8, rows, :], ft, t, 8, 24)):
                pa[t, 0, o, rows, :] = v
            for o, v in enumerate(z_group(lambda i, t=t: e[t, i + 16, rows, :], ft, t, 0, 16)):
                pa[t, 1, o, rows, :] = v

    @pl.loop(0, 9)
    def _(y):
        rows = pl.ds(pl.multiple_of(y * 16, 16), 16)
        for t in range(2):
            for o, v in enumerate(z_group(lambda i, t=t: ec[t, i - 8, rows, :], ct, t, 8, 24)):
                pc[t, 0, o, rows, :] = v
            for o, v in enumerate(z_group(lambda i, t=t: ec[t, i, rows, :], ct, t, 0, 16)):
                pc[t, 1, o, rows, :] = v


def outer_kernel(ft, ct, wref, wcref, pa, pc, zl, zh, sl, sh, fh, fl, fch, fcl, eh, ech, gn):
    w = wref[...]

    def strip(ref, i):
        return jnp.concatenate(
            [
                jnp.concatenate([ref[i], ref[i + 1]], axis=1),
                jnp.concatenate([ref[i + 2], ref[i + 3]], axis=1),
            ],
            axis=0,
        )

    for n, (m, s) in enumerate(((zl, sl), (zh, sh))):

        @pl.loop(0, 8, unroll=4)
        def _(p, n=n, m=m, s=s):
            r = x_block(m[p], strip(s, 4 * p), w)
            for t in range(2):
                eh[t, 8 * n + p, 8:264, :] = r[:, t * 128 : t * 128 + 128]

        @pl.loop(0, 4)
        def _(p, n=n, m=m):
            gn[4 * n + p] = pool(m, p)

    def sides(lo, hi):
        return jnp.concatenate([lo, hi], axis=0)

    def pair(i):
        return jnp.concatenate(
            [jnp.concatenate([sl[i], sh[i]], axis=1), jnp.concatenate([sl[i + 1], sh[i + 1]], axis=1)],
            axis=0,
        )

    r = x_block(
        sides(sl[32:48].reshape(128, 128), sh[32:48].reshape(128, 128)), pair(48), w
    ).reshape(2, 2, 8, 8, 256)
    for n in range(2):
        for t in range(2):
            eh[t, 8 * n : 8 * n + 8, 0:8, :] = r[n, 0, :, :, t * 128 : t * 128 + 128]
            eh[t, 8 * n : 8 * n + 8, 264:272, :] = r[n, 1, :, :, t * 128 : t * 128 + 128]

    wc = wcref[...]
    for n, s in enumerate((sl, sh)):
        for b in range(4):
            near = b >= 2 if n == 0 else b < 2
            if near:
                first = 2 * (b - 2) if n == 0 else 4 + 2 * b
                rows = gn[first : first + 2].reshape(256, 128)
            else:
                first = 50 + 32 * (b if n == 0 else b - 2)
                rows = s[first : first + 32].reshape(256, 128)
            r = x_block(rows, strip(s, 130 + 4 * b), wc).reshape(2, 128, 256)
            for t in range(2):
                ech[t, 8 * n + 2 * b : 8 * n + 2 * b + 2, 8:136, :] = r[:, :, t * 128 : t * 128 + 128]
    r = x_block(
        sides(sl[114:130].reshape(128, 128), sh[114:130].reshape(128, 128)), pair(146), wc
    ).reshape(2, 2, 8, 8, 256)
    for n in range(2):
        for t in range(2):
            ech[t, 8 * n : 8 * n + 8, 0:8, :] = r[n, 0, :, :, t * 128 : t * 128 + 128]
            ech[t, 8 * n : 8 * n + 8, 136:144, :] = r[n, 1, :, :, t * 128 : t * 128 + 128]

    def rest(planes, taps, partial, t, n, rows):
        acc = [partial[t, n, o, rows, :] for o in range(8)]
        first = 16 * n
        return z_group(lambda i: planes[t, 8 * n + i - first, rows, :], taps, t, first, first + 8, acc)

    @pl.loop(0, 17)
    def _(y):
        rows = pl.ds(pl.multiple_of(y * 16, 16), 16)
        for t in range(2):
            for n in range(2):
                put_pair(fh, fl, t, 4 * n, rows, rest(eh, ft, pa, t, n, rows))

    @pl.loop(0, 9)
    def _(y):
        rows = pl.ds(pl.multiple_of(y * 16, 16), 16)
        for t in range(2):
            for n in range(2):
                for o, v in enumerate(rest(ech, ct, pc, t, n, rows)):
                    hi, lo = split(v)
                    cols = slice((o % 2) * 128, (o % 2) * 128 + 128)
                    fch[t, 4 * n + o // 2, rows, cols] = hi
                    fcl[t, 4 * n + o // 2, rows, cols] = lo


def weights_kernel(ft, ct, w, wc, wy, wyc):
    w[...] = x_weights(ft, False)
    wc[...] = x_weights(ct, True)
    for t in range(2):
        wy[:, t * 256 : t * 256 + 256] = y_weights(ft, t, False)
        wyc[:, t * 256 : t * 256 + 256] = y_weights(ct, t, True)


def final_kernel(wyref, wycref, fh, fl, fih, fil, fch, fcl, tp, out_hbm, out, sems):
    wy, wyc = wyref[...], wycref[...]

    def stacked(h, l, index, first, size):
        rows = slice(first, first + size)
        return jnp.concatenate([stack(h[t, index, rows, :], l[t, index, rows, :]) for t in range(2)], axis=0)

    def slab(q, h, l, first):
        for b in range(4):
            top = jnp.concatenate(
                [jnp.broadcast_to(tp[2 * b + k : 2 * b + k + 1, :], (32, 128)) for k in range(2)], axis=0
            )
            common = mm(wyc, stacked(fch, fcl, q, 32 * b, 48))
            even, odd = common[:, 0:128] + top, common[:, 128:256] + top
            for r in range(2):
                res = mm(wy, stacked(h, l, first + r, 64 * b, 80))
                out[4 * q + r, 64 * b : 64 * b + 64, :] = res[:, 0:128] + even
                out[4 * q + 2 + r, 64 * b : 64 * b + 64, :] = res[:, 128:256] + odd

    def leave(q):
        planes = pl.ds(4 * q, 4)
        return pltpu.make_async_copy(out.at[planes], out_hbm.at[planes], sems.at[q])

    @pl.loop(2, 6)
    def _(q):
        slab(q, fih, fil, 2 * q - 4)
        leave(q).start()

    @pl.loop(0, 2)
    def _(n):
        slab(n, fh, fl, 2 * n)
        leave(n).start()
        slab(6 + n, fh, fl, 4 + 2 * n)
        leave(6 + n).start()

    for q in range(8):
        leave(q).wait()


def sds(*shape):
    return jax.ShapeDtypeStruct(shape, f32)


def call(kernel, outs, n_smem, args, scratch=(), flops=0, nbytes=0, grant=12, alias=None, space=VM):
    return pl.pallas_call(
        kernel,
        out_shape=outs,
        in_specs=[SM] * n_smem + [VM] * (len(args) - n_smem),
        out_specs=jax.tree.map(lambda _: space, outs),
        scratch_shapes=scratch,
        compiler_params=pltpu.CompilerParams(vmem_limit_bytes=grant * 1024 * 1024),
        input_output_aliases=alias or {},
        cost_estimate=pl.CostEstimate(flops=flops, bytes_accessed=nbytes, transcendentals=0),
    )(*args)


OFFSETS = {"gx": (0, -1, 1, -4, -3, -2, 2, 3), "gy": (0, -1, 1, 2), "gz": (0, -1, 1, -4, -3, -2, 2, 3)}


def wrapped(d, period):
    d = jnp.abs(d) & (period - 1)
    return jnp.minimum(d, period - d).astype(f32)


def pick(index, values):
    out = jnp.zeros(index.shape, jnp.int32)
    for i, v in enumerate(values):
        out = jnp.where(index == i, v, out)
    return out


def matrix_kernel(k):
    lane = iota((8, 128), 1)
    ys = pick((lane >> 2) & 3, OFFSETS["gy"]) * 8 + iota((8, 128), 0)
    xs = pick(lane >> 4, OFFSETS["gx"]) * 4 + (lane & 3)

    @pl.loop(0, 8)
    def _(y):
        dy = wrapped(y - ys, 32)
        for x in range(4):
            dx = wrapped(x - xs, 32)
            r2 = 1.0 + dy * dy + dx * dx
            for i, off in enumerate(OFFSETS["gz"]):
                dz = float(min(abs(off), 8 - abs(off)))
                k[x, y, i] = 1.0 / (256.0 * jnp.sqrt(r2 + dz * dz))


def top_kernel(k, p3, pm, pp, tp):
    tiles = [p3[0], p3[1], p3[2], pm[1], pm[0], pm[2], pp[1], pp[0]]
    lane = iota((8, 128), 1) >> 5
    out = jnp.zeros((8, 128), f32)
    for x in range(4):
        rows = []
        for y in range(8):
            v = k[x, y, 0] * tiles[0]
            for i in range(1, 8):
                v = v + k[x, y, i] * tiles[i]
            rows.append(jnp.sum(v, axis=0, keepdims=True))
        total = jnp.sum(jnp.concatenate(rows, axis=0), axis=1, keepdims=True)
        out = jnp.where(lane == x, jnp.broadcast_to(total, (8, 128)), out)
    tp[...] = out


def q3_kernel(xlo, xl, xr, q3):
    q3[0:2] = xlo[3:5]
    q3[2:4] = xl[3:5]
    q3[4:6] = xr[3:5]


def p3_kernel(p0, sl, sh, p3):
    p3[0] = p0[...]
    p3[1] = sl[...]
    p3[2] = sh[...]


def body(charges, fine_taps, coarse_taps):
    ft, ct = fine_taps, coarse_taps
    zl = shift(charges[24:32], "gz", 1)
    zh = shift(charges[0:8], "gz", -1)

    g, ylo, yhi, q = call(
        prep_kernel, (sds(16, 128, 128), sds(49, 8, 128), sds(49, 8, 128), sds(8, 128)), 0, (charges,),
        flops=1 << 22, nbytes=6 << 20,
    )
    q2 = shift(q, "gy", 2)
    yl = shift(yhi, "gy", 1)
    yh = shift(ylo, "gy", -1)

    xlo, xhi = call(
        strip_kernel, (sds(NB, 8, 256), sds(NB, 8, 256)), 0, (charges, g),
        flops=1 << 27, nbytes=6 << 20,
    )
    xl = shift(xhi, "gx", 1)
    xr = shift(xlo, "gx", -1)
    clo, chi = call(
        strip_y_kernel, (sds(5, 8, 256), sds(5, 8, 256)), 0, (yl, yh, q, q2),
        flops=1 << 24, nbytes=1 << 20,
    )
    cl = shift(chi, "gx", 1)
    cr = shift(clo, "gx", -1)
    k = call(matrix_kernel, sds(4, 8, 8, 8, 128), 0, (), flops=1 << 24, nbytes=1 << 20)
    wide, tall = (jax.ShapeDtypeStruct(v, bf16) for v in ((64, 512), (512, 256)))
    w, wc, wy, wyc = call(weights_kernel, (tall, tall, wide, wide), 2, (ft, ct), flops=1 << 24, nbytes=1 << 20)
    q3 = call(q3_kernel, sds(6, 8, 256), 0, (clo, cl, cr))
    zlo, zhi = call(
        zstrip_kernel, (sds(NT, 8, 128), sds(NT, 8, 128)), 0, (g, yl, yh, xl, xr, cl, cr),
        flops=1 << 20, nbytes=4 << 20,
    )
    sl = shift(zhi, "gz", 1)
    sh = shift(zlo, "gz", -1)
    qm = shift(q3, "gx", 3)
    qp = shift(q3, "gx", -3)

    e = call(
        own_fine_kernel, sds(2, 32, 272, 128), 0,
        (w, charges, xl, xr), flops=5 << 30, nbytes=16 << 20,
    )
    e = call(
        own_y_kernel, sds(2, 32, 272, 128), 0,
        (e, w, yl, yh, cl, cr), flops=1 << 28, nbytes=1 << 20, alias={0: 0},
    )
    half = jax.ShapeDtypeStruct((2, 8, 272, 256), bf16)
    quarter = jax.ShapeDtypeStruct((2, 8, 144, 256), bf16)
    fih, fil = call(inner_kernel, (half, half), 1, (ft, e), flops=3 << 30, nbytes=16 << 20)
    p0 = call(pack_kernel, sds(8, 128), 0, (q3, qm, qp))
    pl1 = shift(p0, "gz", 1)
    pr1 = shift(p0, "gz", -1)
    pa, pc = call(
        partial_kernel, (sds(2, 2, 8, 272, 128), sds(2, 2, 8, 144, 128)), 2,
        (ft, ct, wc, e, g, yl, yh, xl, xr, cl, cr), scratch=[pltpu.VMEM((2, 16, 144, 128), f32)],
        flops=3 << 30, nbytes=16 << 20,
    )
    p3 = call(p3_kernel, sds(3, 8, 128), 0, (p0, pl1, pr1))
    pm = shift(p3, "gz", 3)
    pp = shift(p3, "gz", -3)
    fh, fl, fch, fcl = call(
        outer_kernel, (half, half, quarter, quarter), 2, (ft, ct, w, wc, pa, pc, zl, zh, sl, sh),
        scratch=[
            pltpu.VMEM((2, 16, 272, 128), f32),
            pltpu.VMEM((2, 16, 144, 128), f32),
            pltpu.VMEM((8, 128, 128), f32),
        ],
        flops=4 << 30, nbytes=16 << 20, grant=16,
    )
    tp = call(top_kernel, sds(8, 128), 0, (k, p3, pm, pp))
    out = call(
        final_kernel, sds(32, 256, 128), 0, (wy, wyc, fh, fl, fih, fil, fch, fcl, tp),
        scratch=[pltpu.VMEM((32, 256, 128), f32), pltpu.SemaphoreType.DMA((8,))],
        flops=2 << 30, nbytes=16 << 20, grant=16, space=pl.BlockSpec(memory_space=pl.ANY),
    )
    return out


def solution(mesh):
    return jax.shard_map(
        body,
        mesh=mesh,
        in_specs=(P("gz", "gy", "gx"), P(), P()),
        out_specs=P("gz", "gy", "gx"),
        check_vma=False,
    )
```

```python
import jax
import jax.numpy as jnp
from jax import lax
from jax.experimental import pallas as pl
from jax.experimental.pallas import tpu as pltpu
from jax.sharding import PartitionSpec as P


f32 = jnp.float32
bf16 = jnp.bfloat16
NB = 40
NT = 148
R = 8
TAPS = 17

VM = pl.BlockSpec(memory_space=pltpu.VMEM)
SM = pl.BlockSpec(memory_space=pltpu.SMEM)


def shift(value, axis, step):
    count = lax.axis_size(axis)
    return lax.ppermute(value, axis, [(i, (i + step) % count) for i in range(count)])


def split(a):
    hi = a.astype(bf16)
    lo = (a - hi.astype(f32)).astype(bf16)
    return hi, lo


def mm(a, b):
    return jnp.dot(a, b, preferred_element_type=f32)


def iota(shape, dim):
    return lax.broadcasted_iota(jnp.int32, shape, dim)


def banded(taps, t, axis, delta):
    out = jnp.zeros(delta.shape, f32)
    for k in range(TAPS):
        out = jnp.where(delta == k, taps[t, axis, k], out)
    return out


def x_weights(taps, coarse):
    sh = 1 if coarse else 0
    scale = 0.125 if coarse else 1.0
    edge = 128 >> sh

    def halves(rows, source):
        cols = iota((rows, 128), 1) >> sh
        return jnp.concatenate(
            [banded(taps, t, 0, source - cols + R) * scale for t in range(2)], axis=1
        )

    hi, lo = split(halves(128, iota((128, 128), 0) >> sh))
    h = iota((16, 128), 0)
    hhi, hlo = split(halves(16, jnp.where(h < 8, h - 8, h - 8 + edge)))
    return jnp.concatenate([hi, hi, lo, hhi, hhi, hlo, jnp.zeros((80, 256), bf16)], axis=0)


def y_weights(taps, t, coarse):
    seg = 48 if coarse else 80
    c = iota((64, 256), 1)
    i = iota((64, 256), 0) >> (1 if coarse else 0)
    j = c - jnp.where(c >= seg, seg, 0) - jnp.where(c >= 2 * seg, seg, 0)
    m = jnp.where(c < 3 * seg, banded(taps, t, 1, j - i), 0.0)
    hi = m.astype(bf16).astype(f32)
    return jnp.where(c < 2 * seg, hi, m - hi).astype(bf16)


def stack(hi, lo):
    pad = jnp.zeros((256 - 3 * hi.shape[0], hi.shape[1]), bf16)
    return jnp.concatenate([hi, lo, hi, pad], axis=0)


def x_block(a, xt, w):
    hi, lo = split(a)
    xhi, xlo = split(xt)
    x3 = jnp.concatenate([xhi, xlo, xhi, jnp.zeros((80, 256), bf16)], axis=0)
    return mm(jnp.concatenate([hi, lo, hi, x3.T], axis=1), w)


def pool(ref, z):
    def half(p):
        return ref[p, pl.ds(0, 128, stride=2), :] + ref[p, pl.ds(1, 128, stride=2), :]

    return half(2 * z) + half(2 * z + 1)


def prep_kernel(d, g, ylo, yhi, own):
    def step(z, acc):
        v = pool(d, z)
        g[z] = v
        return acc + v

    total = lax.fori_loop(0, 16, step, jnp.zeros((128, 128), f32))
    rows = jnp.sum(total.reshape(8, 16, 128), axis=1)
    group = jnp.where((iota((128, 128), 0) >> 5) == iota((128, 128), 1), 0.125, 0.0)
    q = jnp.dot(rows, group, precision=lax.Precision.HIGHEST, preferred_element_type=f32)
    ylo[0:32] = d[:, 0:8, :]
    yhi[0:32] = d[:, 248:256, :]
    ylo[32:48] = g[:, 0:8, :]
    yhi[32:48] = g[:, 120:128, :]
    ylo[48] = q
    yhi[48] = q
    own[...] = q


def put(xlo, xhi, first, sources, coarse):
    width = 32 if coarse else 16
    lane = iota((256, 128), 1)
    tile = None
    for p, v in enumerate(sources):
        if coarse:
            v = v + pltpu.roll(v, 127, 1)
        v = pltpu.roll(v, (width * p + width // 2) % 128, 1)
        tile = v if tile is None else jnp.where(lane >= width * p, v, tile)
    tile = tile.T
    for p in range(len(sources)):
        if coarse:
            rows = [tile[32 * p + 2 * i : 32 * p + 2 * i + 1] for i in range(16)]
            xhi[first + p] = jnp.concatenate(rows[0:8], axis=0)
            xlo[first + p] = jnp.concatenate(rows[8:16], axis=0)
        else:
            xhi[first + p] = tile[16 * p : 16 * p + 8]
            xlo[first + p] = tile[16 * p + 8 : 16 * p + 16]


def strip_kernel(d, g, xlo, xhi):
    for k in range(4):
        put(xlo, xhi, 8 * k, [d[8 * k + p] for p in range(8)], False)
    for k in range(2):
        sources = [g[8 * k + 2 * p : 8 * k + 2 * p + 2].reshape(256, 128) for p in range(4)]
        put(xlo, xhi, 32 + 4 * k, sources, True)


def strip_y_kernel(yl, yh, q, q2, xlo, xhi):
    put(xlo, xhi, 0, [yl[0:32].reshape(256, 128), yh[0:32].reshape(256, 128)], False)
    coarse = jnp.concatenate([yl[32:48].reshape(128, 128), yh[32:48].reshape(128, 128)], axis=0)
    put(xlo, xhi, 2, [coarse], True)
    sides = jnp.concatenate([yl[48], yh[48]], axis=1)
    rest = jnp.concatenate([q[...], q2[...]], axis=1)
    xlo[3] = sides
    xlo[4] = rest
    xhi[3] = sides
    xhi[4] = rest


def pack_kernel(q3, qm, qp, own):
    def quarters(ref, i):
        a, b = ref[2 * i], ref[2 * i + 1]
        return [b[:, 0:4], a[:, 0:4], a[:, 128:132], b[:, 128:132]]

    own[...] = jnp.concatenate(
        sum((quarters(q3, i) for i in range(3)), [])
        + quarters(qm, 1) + quarters(qm, 0) + quarters(qm, 2) + quarters(qp, 0) + quarters(qp, 2),
        axis=1,
    )


def zstrip_kernel(g, yl, yh, xl, xr, cl, cr, zlo, zhi):
    for out, p0, far in ((zlo, 0, 4), (zhi, 24, 8)):
        for p in range(8):
            for s, src in ((0, xl), (1, xr)):
                for half in range(2):
                    out[p * 4 + s * 2 + half] = src[p0 + p, :, half * 128 : half * 128 + 128]
        out[32:40] = yl[p0 : p0 + 8]
        out[40:48] = yh[p0 : p0 + 8]
        for s, src in ((0, cl), (1, cr)):
            a, b = src[0], src[1]
            out[48 + s] = jnp.concatenate([a[:, p0 * 8 : p0 * 8 + 64], b[:, p0 * 8 : p0 * 8 + 64]], axis=1)
        for i in range(4):
            out[50 + 16 * i : 66 + 16 * i] = g[far + i].reshape(16, 8, 128)
        c0 = 0 if p0 == 0 else 8
        out[114:122] = yl[32 + c0 : 40 + c0]
        out[122:130] = yh[32 + c0 : 40 + c0]
        for b in range(4):
            for s, src in ((0, xl), (1, xr)):
                for half in range(2):
                    out[130 + b * 4 + s * 2 + half] = src[32 + c0 // 2 + b, :, half * 128 : half * 128 + 128]
        for s, src in ((0, cl), (1, cr)):
            a = src[2]
            out[146 + s] = jnp.concatenate(
                [a[:, c0 * 8 : c0 * 8 + 64], a[:, 128 + c0 * 8 : 128 + c0 * 8 + 64]], axis=1
            )


def own_fine_kernel(wref, d, xl, xr, e):
    w = wref[...]

    @pl.loop(0, 32, unroll=4)
    def _(z):
        r = x_block(d[z], jnp.concatenate([xl[z], xr[z]], axis=0), w)
        for t in range(2):
            e[t, z, 8:264, :] = r[:, t * 128 : t * 128 + 128]


def own_y_kernel(e_in, wref, yl, yh, cl, cr, e):
    w = wref[...]
    for i, src, row in ((0, yl, 0), (1, yh, 264)):
        strip = jnp.concatenate([cl[i], cr[i]], axis=0)
        r = x_block(src[0:32].reshape(256, 128), strip, w).reshape(32, 8, 256)
        for t in range(2):
            e[t, :, row : row + 8, :] = r[:, :, t * 128 : t * 128 + 128]


def own_coarse(wcref, g, yl, yh, xl, xr, cl, cr, ec):
    def strip(i):
        return jnp.concatenate([xl[i], xr[i]], axis=0)

    wc = wcref[...]

    @pl.loop(0, 8, unroll=4)
    def _(b):
        r = x_block(g[pl.ds(2 * b, 2)].reshape(256, 128), strip(32 + b), wc).reshape(2, 128, 256)
        for t in range(2):
            ec[t, pl.ds(2 * b, 2), 8:136, :] = r[:, :, t * 128 : t * 128 + 128]

    r = x_block(
        jnp.concatenate([yl[32:48].reshape(128, 128), yh[32:48].reshape(128, 128)], axis=0),
        jnp.concatenate([cl[2], cr[2]], axis=0), wc,
    ).reshape(2, 16, 8, 256)
    for t in range(2):
        ec[t, :, 0:8, :] = r[0, :, :, t * 128 : t * 128 + 128]
        ec[t, :, 136:144, :] = r[1, :, :, t * 128 : t * 128 + 128]


def z_group(planes, taps, t, first, last, acc=None):
    w = [jnp.full((8, 128), taps[t, 2, k], f32) for k in range(TAPS)]
    w = [jnp.concatenate([v, v], axis=0) for v in w]
    acc = [None] * 8 if acc is None else list(acc)
    for i in range(first, last):
        v = planes(i)
        for o in range(8):
            k = i - o
            if 0 <= k < TAPS:
                acc[o] = w[k] * v if acc[o] is None else acc[o] + w[k] * v
    return acc


def put_pair(hi_ref, lo_ref, t, first, rows, values):
    for z, v in enumerate(values):
        q, l, r = z // 4, z // 2 % 2, z % 2
        hi, lo = split(v)
        hi_ref[t, first + 2 * q + r, rows, l * 128 : l * 128 + 128] = hi
        lo_ref[t, first + 2 * q + r, rows, l * 128 : l * 128 + 128] = lo


def inner_kernel(ft, e, fih, fil):
    @pl.loop(0, 17)
    def _(y):
        rows = pl.ds(pl.multiple_of(y * 16, 16), 16)
        for t in range(2):
            for n in range(2):

                def plane(i, t=t, n=n):
                    return e[t, i + 8 * n, rows, :]

                put_pair(fih, fil, t, 4 * n, rows, z_group(plane, ft, t, 0, 24))


def partial_kernel(ft, ct, wcref, e, g, yl, yh, xl, xr, cl, cr, pa, pc, ec):
    own_coarse(wcref, g, yl, yh, xl, xr, cl, cr, ec)

    @pl.loop(0, 17)
    def _(y):
        rows = pl.ds(pl.multiple_of(y * 16, 16), 16)
        for t in range(2):
            for o, v in enumerate(z_group(lambda i, t=t: e[t, i - 8, rows, :], ft, t, 8, 24)):
                pa[t, 0, o, rows, :] = v
            for o, v in enumerate(z_group(lambda i, t=t: e[t, i + 16, rows, :], ft, t, 0, 16)):
                pa[t, 1, o, rows, :] = v

    @pl.loop(0, 9)
    def _(y):
        rows = pl.ds(pl.multiple_of(y * 16, 16), 16)
        for t in range(2):
            for o, v in enumerate(z_group(lambda i, t=t: ec[t, i - 8, rows, :], ct, t, 8, 24)):
                pc[t, 0, o, rows, :] = v
            for o, v in enumerate(z_group(lambda i, t=t: ec[t, i, rows, :], ct, t, 0, 16)):
                pc[t, 1, o, rows, :] = v


def outer_kernel(ft, ct, wref, wcref, pa, pc, zl, zh, sl, sh, fh, fl, fch, fcl, eh, ech, gn):
    w = wref[...]

    def strip(ref, i):
        return jnp.concatenate(
            [
                jnp.concatenate([ref[i], ref[i + 1]], axis=1),
                jnp.concatenate([ref[i + 2], ref[i + 3]], axis=1),
            ],
            axis=0,
        )

    for n, (m, s) in enumerate(((zl, sl), (zh, sh))):

        @pl.loop(0, 8, unroll=4)
        def _(p, n=n, m=m, s=s):
            r = x_block(m[p], strip(s, 4 * p), w)
            for t in range(2):
                eh[t, 8 * n + p, 8:264, :] = r[:, t * 128 : t * 128 + 128]

        @pl.loop(0, 4)
        def _(p, n=n, m=m):
            gn[4 * n + p] = pool(m, p)

    def sides(lo, hi):
        return jnp.concatenate([lo, hi], axis=0)

    def pair(i):
        return jnp.concatenate(
            [jnp.concatenate([sl[i], sh[i]], axis=1), jnp.concatenate([sl[i + 1], sh[i + 1]], axis=1)],
            axis=0,
        )

    r = x_block(
        sides(sl[32:48].reshape(128, 128), sh[32:48].reshape(128, 128)), pair(48), w
    ).reshape(2, 2, 8, 8, 256)
    for n in range(2):
        for t in range(2):
            eh[t, 8 * n : 8 * n + 8, 0:8, :] = r[n, 0, :, :, t * 128 : t * 128 + 128]
            eh[t, 8 * n : 8 * n + 8, 264:272, :] = r[n, 1, :, :, t * 128 : t * 128 + 128]

    wc = wcref[...]
    for n, s in enumerate((sl, sh)):
        for b in range(4):
            near = b >= 2 if n == 0 else b < 2
            if near:
                first = 2 * (b - 2) if n == 0 else 4 + 2 * b
                rows = gn[first : first + 2].reshape(256, 128)
            else:
                first = 50 + 32 * (b if n == 0 else b - 2)
                rows = s[first : first + 32].reshape(256, 128)
            r = x_block(rows, strip(s, 130 + 4 * b), wc).reshape(2, 128, 256)
            for t in range(2):
                ech[t, 8 * n + 2 * b : 8 * n + 2 * b + 2, 8:136, :] = r[:, :, t * 128 : t * 128 + 128]
    r = x_block(
        sides(sl[114:130].reshape(128, 128), sh[114:130].reshape(128, 128)), pair(146), wc
    ).reshape(2, 2, 8, 8, 256)
    for n in range(2):
        for t in range(2):
            ech[t, 8 * n : 8 * n + 8, 0:8, :] = r[n, 0, :, :, t * 128 : t * 128 + 128]
            ech[t, 8 * n : 8 * n + 8, 136:144, :] = r[n, 1, :, :, t * 128 : t * 128 + 128]

    def rest(planes, taps, partial, t, n, rows):
        acc = [partial[t, n, o, rows, :] for o in range(8)]
        first = 16 * n
        return z_group(lambda i: planes[t, 8 * n + i - first, rows, :], taps, t, first, first + 8, acc)

    @pl.loop(0, 17)
    def _(y):
        rows = pl.ds(pl.multiple_of(y * 16, 16), 16)
        for t in range(2):
            for n in range(2):
                put_pair(fh, fl, t, 4 * n, rows, rest(eh, ft, pa, t, n, rows))

    @pl.loop(0, 9)
    def _(y):
        rows = pl.ds(pl.multiple_of(y * 16, 16), 16)
        for t in range(2):
            for n in range(2):
                for o, v in enumerate(rest(ech, ct, pc, t, n, rows)):
                    hi, lo = split(v)
                    cols = slice((o % 2) * 128, (o % 2) * 128 + 128)
                    fch[t, 4 * n + o // 2, rows, cols] = hi
                    fcl[t, 4 * n + o // 2, rows, cols] = lo


def weights_kernel(ft, ct, w, wc, wy, wyc):
    w[...] = x_weights(ft, False)
    wc[...] = x_weights(ct, True)
    for t in range(2):
        wy[:, t * 256 : t * 256 + 256] = y_weights(ft, t, False)
        wyc[:, t * 256 : t * 256 + 256] = y_weights(ct, t, True)


def final_kernel(wyref, wycref, fh, fl, fih, fil, fch, fcl, tp, out_hbm, out, sems):
    wy, wyc = wyref[...], wycref[...]

    def stacked(h, l, index, first, size):
        rows = slice(first, first + size)
        return jnp.concatenate([stack(h[t, index, rows, :], l[t, index, rows, :]) for t in range(2)], axis=0)

    def slab(q, h, l, first):
        for b in range(4):
            top = jnp.concatenate(
                [jnp.broadcast_to(tp[2 * b + k : 2 * b + k + 1, :], (32, 128)) for k in range(2)], axis=0
            )
            common = mm(wyc, stacked(fch, fcl, q, 32 * b, 48))
            even, odd = common[:, 0:128] + top, common[:, 128:256] + top
            for r in range(2):
                res = mm(wy, stacked(h, l, first + r, 64 * b, 80))
                out[4 * q + r, 64 * b : 64 * b + 64, :] = res[:, 0:128] + even
                out[4 * q + 2 + r, 64 * b : 64 * b + 64, :] = res[:, 128:256] + odd

    def leave(q):
        planes = pl.ds(4 * q, 4)
        return pltpu.make_async_copy(out.at[planes], out_hbm.at[planes], sems.at[q])

    @pl.loop(2, 6)
    def _(q):
        slab(q, fih, fil, 2 * q - 4)
        leave(q).start()

    @pl.loop(0, 2)
    def _(n):
        slab(n, fh, fl, 2 * n)
        leave(n).start()
        slab(6 + n, fh, fl, 4 + 2 * n)
        leave(6 + n).start()

    for q in range(8):
        leave(q).wait()


def sds(*shape):
    return jax.ShapeDtypeStruct(shape, f32)


def call(kernel, outs, n_smem, args, scratch=(), flops=0, nbytes=0, grant=12, alias=None, space=VM):
    return pl.pallas_call(
        kernel,
        out_shape=outs,
        in_specs=[SM] * n_smem + [VM] * (len(args) - n_smem),
        out_specs=jax.tree.map(lambda _: space, outs),
        scratch_shapes=scratch,
        compiler_params=pltpu.CompilerParams(vmem_limit_bytes=grant * 1024 * 1024),
        input_output_aliases=alias or {},
        cost_estimate=pl.CostEstimate(flops=flops, bytes_accessed=nbytes, transcendentals=0),
    )(*args)


OFFSETS = {"gx": (0, -1, 1, -4, -3, -2, 2, 3), "gy": (0, -1, 1, 2), "gz": (0, -1, 1, -4, -3, -2, 2, 3)}


def wrapped(d, period):
    d = jnp.abs(d) & (period - 1)
    return jnp.minimum(d, period - d).astype(f32)


def pick(index, values):
    out = jnp.zeros(index.shape, jnp.int32)
    for i, v in enumerate(values):
        out = jnp.where(index == i, v, out)
    return out


def matrix_kernel(k):
    lane = iota((8, 128), 1)
    ys = pick((lane >> 2) & 3, OFFSETS["gy"]) * 8 + iota((8, 128), 0)
    xs = pick(lane >> 4, OFFSETS["gx"]) * 4 + (lane & 3)

    @pl.loop(0, 8)
    def _(y):
        dy = wrapped(y - ys, 32)
        for x in range(4):
            dx = wrapped(x - xs, 32)
            r2 = 1.0 + dy * dy + dx * dx
            for i, off in enumerate(OFFSETS["gz"]):
                dz = float(min(abs(off), 8 - abs(off)))
                k[x, y, i] = 1.0 / (256.0 * jnp.sqrt(r2 + dz * dz))


def top_kernel(k, p3, pm, pp, tp):
    tiles = [p3[0], p3[1], p3[2], pm[1], pm[0], pm[2], pp[0], pp[2]]
    lane = iota((8, 128), 1) >> 5
    out = jnp.zeros((8, 128), f32)
    for x in range(4):
        rows = []
        for y in range(8):
            v = k[x, y, 0] * tiles[0]
            for i in range(1, 8):
                v = v + k[x, y, i] * tiles[i]
            rows.append(jnp.sum(v, axis=0, keepdims=True))
        total = jnp.sum(jnp.concatenate(rows, axis=0), axis=1, keepdims=True)
        out = jnp.where(lane == x, jnp.broadcast_to(total, (8, 128)), out)
    tp[...] = out


def q3_kernel(xlo, xl, xr, q3):
    q3[0:2] = xlo[3:5]
    q3[2:4] = xl[3:5]
    q3[4:6] = xr[3:5]


def p3_kernel(p0, sl, sh, p3):
    p3[0] = p0[...]
    p3[1] = sl[...]
    p3[2] = sh[...]


def body(charges, fine_taps, coarse_taps):
    ft, ct = fine_taps, coarse_taps
    zl = shift(charges[24:32], "gz", 1)
    zh = shift(charges[0:8], "gz", -1)

    g, ylo, yhi, q = call(
        prep_kernel, (sds(16, 128, 128), sds(49, 8, 128), sds(49, 8, 128), sds(8, 128)), 0, (charges,),
        flops=1 << 22, nbytes=6 << 20,
    )
    q2 = shift(q, "gy", 2)
    yl = shift(yhi, "gy", 1)
    yh = shift(ylo, "gy", -1)

    xlo, xhi = call(
        strip_kernel, (sds(NB, 8, 256), sds(NB, 8, 256)), 0, (charges, g),
        flops=1 << 27, nbytes=6 << 20,
    )
    xl = shift(xhi, "gx", 1)
    xr = shift(xlo, "gx", -1)
    clo, chi = call(
        strip_y_kernel, (sds(5, 8, 256), sds(5, 8, 256)), 0, (yl, yh, q, q2),
        flops=1 << 24, nbytes=1 << 20,
    )
    cl = shift(chi, "gx", 1)
    cr = shift(clo, "gx", -1)
    k = call(matrix_kernel, sds(4, 8, 8, 8, 128), 0, (), flops=1 << 24, nbytes=1 << 20)
    wide, tall = (jax.ShapeDtypeStruct(v, bf16) for v in ((64, 512), (512, 256)))
    w, wc, wy, wyc = call(weights_kernel, (tall, tall, wide, wide), 2, (ft, ct), flops=1 << 24, nbytes=1 << 20)
    q3 = call(q3_kernel, sds(6, 8, 256), 0, (clo, cl, cr))
    zlo, zhi = call(
        zstrip_kernel, (sds(NT, 8, 128), sds(NT, 8, 128)), 0, (g, yl, yh, xl, xr, cl, cr),
        flops=1 << 20, nbytes=4 << 20,
    )
    sl = shift(zhi, "gz", 1)
    sh = shift(zlo, "gz", -1)
    qm = shift(q3, "gx", 3)
    qp = shift(q3, "gx", -2)

    e = call(
        own_fine_kernel, sds(2, 32, 272, 128), 0,
        (w, charges, xl, xr), flops=5 << 30, nbytes=16 << 20,
    )
    e = call(
        own_y_kernel, sds(2, 32, 272, 128), 0,
        (e, w, yl, yh, cl, cr), flops=1 << 28, nbytes=1 << 20, alias={0: 0},
    )
    half = jax.ShapeDtypeStruct((2, 8, 272, 256), bf16)
    quarter = jax.ShapeDtypeStruct((2, 8, 144, 256), bf16)
    fih, fil = call(inner_kernel, (half, half), 1, (ft, e), flops=3 << 30, nbytes=16 << 20)
    p0 = call(pack_kernel, sds(8, 128), 0, (q3, qm, qp))
    pl1 = shift(p0, "gz", 1)
    pr1 = shift(p0, "gz", -1)
    pa, pc = call(
        partial_kernel, (sds(2, 2, 8, 272, 128), sds(2, 2, 8, 144, 128)), 2,
        (ft, ct, wc, e, g, yl, yh, xl, xr, cl, cr), scratch=[pltpu.VMEM((2, 16, 144, 128), f32)],
        flops=3 << 30, nbytes=16 << 20,
    )
    p3 = call(p3_kernel, sds(3, 8, 128), 0, (p0, pl1, pr1))
    pm = shift(p3, "gz", 3)
    pp = shift(p3, "gz", -2)
    fh, fl, fch, fcl = call(
        outer_kernel, (half, half, quarter, quarter), 2, (ft, ct, w, wc, pa, pc, zl, zh, sl, sh),
        scratch=[
            pltpu.VMEM((2, 16, 272, 128), f32),
            pltpu.VMEM((2, 16, 144, 128), f32),
            pltpu.VMEM((8, 128, 128), f32),
        ],
        flops=4 << 30, nbytes=16 << 20, grant=16,
    )
    tp = call(top_kernel, sds(8, 128), 0, (k, p3, pm, pp))
    out = call(
        final_kernel, sds(32, 256, 128), 0, (wy, wyc, fh, fl, fih, fil, fch, fcl, tp),
        scratch=[pltpu.VMEM((32, 256, 128), f32), pltpu.SemaphoreType.DMA((8,))],
        flops=2 << 30, nbytes=16 << 20, grant=16, space=pl.BlockSpec(memory_space=pl.ANY),
    )
    return out


def solution(mesh):
    return jax.shard_map(
        body,
        mesh=mesh,
        in_specs=(P("gz", "gy", "gx"), P(), P()),
        out_specs=P("gz", "gy", "gx"),
        check_vma=False,
    )
```
